512 devices in a mesh: gx: 16 (over z), gz: 32 (over x, y, core).
Axes of the slice: x: 4, y: 4, z: 16, core: 2. Of those that a mesh axis runs over, the one named last changes fastest.
Arguments:
- velocity: float32 [3, 4096, 1, 4096], P(None, 'gx', None, 'gz'), may hold values from -6 to 6
Outputs:
- advection: float32 [3, 4096, 1, 4096], P(None, 'gx', None, 'gz')
The draws below stay inside these ranges and needn't reach their ends.
All inputs are finite; a program needn't handle non-finite values.
Results may differ from the reference program's by a relative error of at most 0.00013.
Values sent between devices are 32-bit elements; how exact they have to be, the bound alone decides.
A program may use at most 64 MiB of HBM per device.

```python
import jax
import jax.numpy as jnp
from jax import lax

NX = 4096
NZ = 4096
YP = 1


def steps_of(key, shape, shards, least, top_value):
    def one(position, parts):
        draws = jax.random.uniform(jax.random.fold_in(jax.random.fold_in(key, 6), position), (parts,), jnp.float32, least / len(shards), top_value / len(shards))
        return jnp.repeat(jnp.exp(draws), shape[position] // parts).reshape((-1,) + (1,) * (len(shape) - position - 1))

    loudness = one(*shards[0])
    for cut in shards[1:]:
        loudness = loudness * one(*cut)
    return loudness


def scatter_about(own_key, shape, deviation, bound, split=(), kind=jnp.bfloat16):
    entries = deviation * jax.random.normal(own_key, shape, jnp.float32)
    if split:
        entries = entries * steps_of(own_key, shape, split, -0.22, 0.18)
    return jnp.clip(entries, -bound, bound).astype(kind)


def setup_inputs(seed: int = 0) -> dict:
    key_list = jax.random.split(jax.random.key(seed), 2)
    return {
        "velocity": scatter_about(key_list[0], (3, NX, YP, NZ), 1.0, 6.0, ((1, 16), (3, 32)), jnp.float32),
    }


ALPHA_D = 1.0 / 3.0
COEF_A = 14.0 / 9.0
COEF_B = 1.0 / 9.0
ALPHA_F = 0.49


def filter_coefficients():
    return ((11.0 + 10.0 * ALPHA_F) / 16.0, (15.0 + 34.0 * ALPHA_F) / 32.0,
            (-3.0 + 6.0 * ALPHA_F) / 16.0, (1.0 - 2.0 * ALPHA_F) / 32.0)


def shifted(values, offset, direction):
    return jnp.roll(values, -offset, axis=direction)


def circulant_solve(rhs, alpha, direction):
    length = rhs.shape[direction]
    spectrum = jnp.fft.rfft(rhs, axis=direction)
    wavenums = jnp.arange(length // 2 + 1, dtype=jnp.float32)
    symbol = 1.0 + 2.0 * alpha * jnp.cos(2.0 * jnp.pi * wavenums / length)
    dims_list = [1] * rhs.ndim
    dims_list[direction] = length // 2 + 1
    return jnp.fft.irfft(spectrum / symbol.reshape(dims_list), n=length, axis=direction).astype(rhs.dtype)


def slope(values, direction):
    rhs = COEF_A * 0.5 * (shifted(values, 1, direction) - shifted(values, -1, direction))
    rhs = rhs + COEF_B * 0.25 * (shifted(values, 2, direction) - shifted(values, -2, direction))
    return circulant_solve(rhs, ALPHA_D, direction)


def smooth(values, direction):
    coefficients = filter_coefficients()
    rhs = coefficients[0] * values
    for offset in range(1, 4):
        rhs = rhs + 0.5 * coefficients[offset] * (shifted(values, offset, direction) + shifted(values, -offset, direction))
    return circulant_solve(rhs, ALPHA_F, direction)


def one_plane(velocity_plane):
    along_x = velocity_plane[0:1]
    along_z = velocity_plane[2:3]
    x_terms = slope(along_x * velocity_plane, 1) + along_x * slope(velocity_plane, 1)
    z_terms = slope(along_z * velocity_plane, 2) + along_z * slope(velocity_plane, 2)
    return -smooth(0.5 * (x_terms + z_terms), 1)


def reference(velocity):
    planes = lax.map(one_plane, jnp.moveaxis(velocity, 2, 0))
    return jnp.moveaxis(planes, 0, 2)
```

```python
import jax
import jax.numpy as jnp
import ml_dtypes
import numpy as np
from jax import lax
from jax.experimental import pallas as pl
from jax.experimental.pallas import tpu as pltpu
from jax.sharding import PartitionSpec as P

ALPHA_D = 1.0 / 3.0
COEF_A = 14.0 / 9.0
COEF_B = 1.0 / 9.0
ALPHA_F = 0.49
LX = 256
LZ = 128
EDGE = 96
MESH = pl.DeviceIdType.MESH


def filter_coefficients():
    return (
        (11.0 + 10.0 * ALPHA_F) / 16.0,
        (15.0 + 34.0 * ALPHA_F) / 32.0,
        (-3.0 + 6.0 * ALPHA_F) / 16.0,
        (1.0 - 2.0 * ALPHA_F) / 32.0,
    )


def line_kernel(alpha, stencil):
    root = np.sqrt(1.0 - 4.0 * alpha * alpha)
    rate = (-1.0 + root) / (2.0 * alpha)

    def response(n):
        n = np.asarray(n)
        return sum(s * rate ** np.abs(n + m) / root for m, s in stencil.items())

    far = max(stencil)
    return response, rate, float(response(far) / rate**far)


def slope_kernel():
    a, b = 0.5 * COEF_A, 0.25 * COEF_B
    response, rate, factor = line_kernel(ALPHA_D, {1: 0.5 * a, -1: -0.5 * a, 2: 0.5 * b, -2: -0.5 * b})
    return response, rate, factor, float(response(1)) - factor * rate


def smooth_kernel():
    c = filter_coefficients()
    stencil = {0: -c[0]}
    for n in (1, 2, 3):
        stencil[n] = stencil[-n] = -0.5 * c[n]
    response, rate, factor = line_kernel(ALPHA_F, stencil)
    near = [float(response(n)) - factor * rate**n for n in (1, 2)]
    return response, rate, factor, near


def halves(table):
    table = np.asarray(table, np.float32)
    high = table.astype(ml_dtypes.bfloat16)
    low = (table - high.astype(np.float32)).astype(ml_dtypes.bfloat16)
    return high, low


def tables():
    response, rate, factor, near = slope_kernel()
    i = np.arange(LX)
    k = np.arange(LZ)
    rows = np.zeros((LX + 16, LX))
    rows[:LX] = response(i[:, None] - i[None, :])
    rows[LX] = factor * rate ** (LX - i)
    rows[LX + 1] = -factor * rate ** (i + 1.0)
    slope_x = np.concatenate(halves(rows))
    high, low = halves(response(k[None, :] - k[:, None]))
    slope_z = np.block([[high, low], [high, np.zeros_like(low)]])
    sends = np.zeros((32, 6, LZ))
    for f in range(6):
        sends[f, f] = factor * rate ** (LZ - k)
        sends[6 + f, f, LZ - 1] = 1.0
        sends[16 + f, f] = -factor * rate ** (k + 1.0)
        sends[22 + f, f, 0] = 1.0
    high, low = halves(sends)
    none = np.zeros_like(low)
    send_z = np.concatenate(
        [np.concatenate([high, high], axis=2), np.concatenate([low, none], axis=2)]
    ).reshape(64, 6 * 2 * LZ)
    spread = np.zeros((32, 6, LZ))
    for f in range(6):
        spread[f, f] = rate**k
        spread[6 + f, f, 0] = near
        spread[16 + f, f] = rate ** (LZ - 1.0 - k)
        spread[22 + f, f, LZ - 1] = -near
    high, low = halves(spread.reshape(32, 6 * LZ))
    spread_z = np.concatenate([high, high, low])
    fade_x = np.zeros((2, EDGE, LZ), np.float32)
    fade_x[0] = (rate ** i[:EDGE])[:, None]
    fade_x[1] = fade_x[0, ::-1]
    response, rate, factor, _ = smooth_kernel()
    smooth_x = np.concatenate(halves(response(i[:, None] - i[None, :])))
    fade_f = np.zeros((2, LX, LZ), np.float32)
    fade_f[0] = (rate**i)[:, None]
    fade_f[1] = fade_f[0, ::-1]
    return send_z, slope_x, slope_z, spread_z, fade_x, fade_f, smooth_x


def split(values):
    high = values.astype(jnp.bfloat16)
    low = (values - high.astype(jnp.float32)).astype(jnp.bfloat16)
    return high, low


def dot(a, b, dims=((1,), (0,))):
    return lax.dot_general(a, b, (dims, ((), ())), preferred_element_type=jnp.float32)


def kernel(
    counts,
    velocity_hbm, send_z_hbm, slope_x_hbm, slope_z_hbm, spread_z_hbm, fade_x_hbm, fade_f_hbm, smooth_x_hbm,
    out_hbm,
    v, send_z, slope_x, slope_z, spread_z, fade_x, fade_f, smooth_x,
    fields, part_x, h, h_halves, out,
    z_out, z_in, x_out, x_in, f_out, f_in,
    load_sem, store_sem, send_sem, recv_sem,
):
    nx, nz = counts
    gx, gz = lax.axis_index("gx"), lax.axis_index("gz")
    x_next, x_prev = lax.rem(gx + 1, nx), lax.rem(gx + nx - 1, nx)
    z_next, z_prev = lax.rem(gz + 1, nz), lax.rem(gz + nz - 1, nz)
    sides_z = ((gx, z_next), (gx, z_prev))
    sides_x = ((x_next, gz), (x_prev, gz))

    barrier = pltpu.get_barrier_semaphore()
    for side in sides_z + sides_x:
        pl.semaphore_signal(barrier, inc=1, device_id=side, device_id_type=MESH)

    loads = [
        pltpu.make_async_copy(src, dst, load_sem.at[n])
        for n, (src, dst) in enumerate(
            (
                (velocity_hbm, v),
                (send_z_hbm, send_z),
                (slope_x_hbm, slope_x),
                (slope_z_hbm, slope_z),
                (spread_z_hbm, spread_z),
                (fade_x_hbm, fade_x),
                (fade_f_hbm, fade_f),
                (smooth_x_hbm, smooth_x),
            )
        )
    ]
    for load in loads:
        load.start()

    loads[0].wait()
    u, w = v[0], v[2]
    for n, field in enumerate((u * u, u * v[1], u, v[1], w, u * w, w * v[1], w * w)):
        high, low = split(field)
        fields[:, n * 256 : n * 256 + 128] = high
        fields[:, n * 256 + 128 : n * 256 + 256] = low

    loads[1].wait()
    both = dot(send_z[...], fields[:, 512:], ((1,), (1,)))
    z_out[...] = both[:32] + both[32:]
    pl.semaphore_wait(barrier, 4)
    copies_z = []
    for n, side in enumerate(sides_z):
        copies_z.append(
            pltpu.make_async_remote_copy(
                src_ref=z_out.at[pl.ds(16 * n, 16)],
                dst_ref=z_in.at[pl.ds(16 * n, 16)],
                send_sem=send_sem.at[n],
                recv_sem=recv_sem.at[n],
                device_id=side,
                device_id_type=MESH,
            )
        )
        copies_z[-1].start()

    loads[2].wait()
    for f in range(6):
        full = dot(slope_x[...], fields[:, f * 256 : f * 256 + 256])
        part = full[: LX + 16, :128] + full[: LX + 16, 128:] + full[LX + 16 :, :128]
        part_x[f] = part[:LX]
        x_out[0, f : f + 1] = part[LX : LX + 1]
        x_out[1, f : f + 1] = part[LX + 1 : LX + 2]
    for side, row in ((0, LX - 1), (1, 0)):
        ur, vr, wr = v[0, row : row + 1], v[1, row : row + 1], v[2, row : row + 1]
        for f, value in enumerate((ur * ur, ur * vr, ur, vr, wr, ur * wr)):
            x_out[side, 6 + f : 7 + f] = value
    copies_x = []
    for n, side in enumerate(sides_x):
        copies_x.append(
            pltpu.make_async_remote_copy(
                src_ref=x_out.at[n],
                dst_ref=x_in.at[n],
                send_sem=send_sem.at[2 + n],
                recv_sem=recv_sem.at[2 + n],
                device_id=side,
                device_id_type=MESH,
            )
        )
        copies_x[-1].start()

    loads[3].wait()
    flat = (0, 1, 5)
    for c in range(3):
        total = part_x[flat[c]] + u * part_x[2 + c]
        for f, factor in ((2 + c, w), (5 + c, None)):
            full = dot(fields[:, f * 256 : f * 256 + 256], slope_z[...])
            part = full[:, :128] + full[:, 128:]
            total = total + (part if factor is None else factor * part)
        h[c] = total

    for load in loads[4:]:
        load.wait()
    _, _, _, near_d = slope_kernel()
    first = lax.broadcasted_iota(jnp.int32, (8, LZ), 0) == 0
    last = lax.broadcasted_iota(jnp.int32, (8, LZ), 0) == 7
    for copy in copies_x:
        copy.wait()
    for c in range(3):
        uv, vc = flat[c], 2 + c
        rows = slice(0, EDGE)
        h[c, rows] += fade_x[0] * (x_in[0, uv : uv + 1] + v[0, rows] * x_in[0, vc : vc + 1])
        near = x_in[0, 6 + uv : 7 + uv] + v[0, 0:8] * x_in[0, 6 + vc : 7 + vc]
        h[c, 0:8] += jnp.where(first, near_d * near, 0.0)
        rows = slice(LX - EDGE, LX)
        h[c, rows] += fade_x[1] * (x_in[1, uv : uv + 1] + v[0, rows] * x_in[1, vc : vc + 1])
        near = x_in[1, 6 + uv : 7 + uv] + v[0, LX - 8 : LX] * x_in[1, 6 + vc : 7 + vc]
        h[c, LX - 8 : LX] -= jnp.where(last, near_d * near, 0.0)

    for copy in copies_z:
        copy.wait()
    high, low = split(z_in[...])
    spread = dot(jnp.concatenate([high, low, high]), spread_z[...], ((0,), (0,)))
    for c in range(3):
        at, to = (3 + c) * 128, c * 128
        h[c] += spread[:, at : at + 128] + w * spread[:, to : to + 128]

    for c in range(3):
        for side, (a, b) in enumerate(((LX - 1, LX - 2), (0, 1))):
            f_out[side, c : c + 1] = jnp.sum(fade_f[1 - side] * h[c], axis=0, keepdims=True)
            f_out[side, 3 + c : 4 + c] = h[c, a : a + 1]
            f_out[side, 6 + c : 7 + c] = h[c, b : b + 1]
    copies_f = []
    for n, side in enumerate(sides_x):
        copies_f.append(
            pltpu.make_async_remote_copy(
                src_ref=f_out.at[n],
                dst_ref=f_in.at[n],
                send_sem=send_sem.at[4 + n],
                recv_sem=recv_sem.at[4 + n],
                device_id=side,
                device_id_type=MESH,
            )
        )
        copies_f[-1].start()

    for c in range(3):
        high, low = split(h[c])
        h_halves[c, :, :128] = high
        h_halves[c, :, 128:] = low
        full = dot(smooth_x[...], h_halves[c])
        out[c] = full[:LX, :128] + full[:LX, 128:] + full[LX:, :128]

    _, rate, factor, (near1, near2) = smooth_kernel()
    row = lax.broadcasted_iota(jnp.int32, (8, LZ), 0)
    for copy in copies_f:
        copy.wait()
    stores = []
    for c in range(3):
        scale = rate * factor
        below, above = scale * f_in[0, c : c + 1], scale * f_in[1, c : c + 1]
        out[c] += fade_f[0] * below + fade_f[1] * above
        for side, start, end0, end1 in ((0, 0, 0, 1), (1, LX - 8, 7, 6)):
            cell1, cell2 = f_in[side, 3 + c : 4 + c], f_in[side, 6 + c : 7 + c]
            out[c, start : start + 8] += jnp.where(row == end0, near1 * cell1 + near2 * cell2, 0.0) + jnp.where(
                row == end1, near2 * cell1, 0.0
            )
        stores.append(pltpu.make_async_copy(out.at[c], out_hbm.at[c], store_sem.at[c]))
        stores[-1].start()
    for store in stores:
        store.wait()


def per_device(counts, velocity):
    operands = [jnp.asarray(t) for t in tables()]
    bf16, f32 = jnp.bfloat16, jnp.float32
    flat = velocity.reshape(3, LX, LZ)
    out = pl.pallas_call(
        lambda *refs: kernel(counts, *refs),
        out_shape=jax.ShapeDtypeStruct((3, LX, LZ), f32),
        in_specs=[pl.BlockSpec(memory_space=pl.ANY)] * 8,
        out_specs=pl.BlockSpec(memory_space=pl.ANY),
        scratch_shapes=[pltpu.VMEM((3, LX, LZ), f32)]
        + [pltpu.VMEM(t.shape, t.dtype) for t in operands]
        + [
            pltpu.VMEM((LX, 8 * 256), bf16),
            pltpu.VMEM((6, LX, LZ), f32),
            pltpu.VMEM((3, LX, LZ), f32),
            pltpu.VMEM((3, LX, 2 * LZ), bf16),
            pltpu.VMEM((3, LX, LZ), f32),
            pltpu.VMEM((32, LX), f32),
            pltpu.VMEM((32, LX), f32),
            pltpu.VMEM((2, 16, LZ), f32),
            pltpu.VMEM((2, 16, LZ), f32),
            pltpu.VMEM((2, 16, LZ), f32),
            pltpu.VMEM((2, 16, LZ), f32),
            pltpu.SemaphoreType.DMA((8,)),
            pltpu.SemaphoreType.DMA((3,)),
            pltpu.SemaphoreType.DMA((6,)),
            pltpu.SemaphoreType.DMA((6,)),
        ],
        compiler_params=pltpu.CompilerParams(collective_id=0, has_side_effects=True, vmem_limit_bytes=32 * 2**20),
    )(flat, *operands)
    return out.reshape(3, LX, 1, LZ)


def solution(mesh):
    counts = (mesh.shape["gx"], mesh.shape["gz"])
    return jax.shard_map(
        lambda velocity: per_device(counts, velocity),
        mesh=mesh,
        in_specs=(P(None, "gx", None, "gz"),),
        out_specs=P(None, "gx", None, "gz"),
        check_vma=False,
    )
```

```python
import jax
import jax.numpy as jnp
import ml_dtypes
import numpy as np
from jax import lax
from jax.experimental import pallas as pl
from jax.experimental.pallas import tpu as pltpu
from jax.sharding import PartitionSpec as P

ALPHA_D = 1.0 / 3.0
COEF_A = 14.0 / 9.0
COEF_B = 1.0 / 9.0
ALPHA_F = 0.49
LX = 256
LZ = 128
EDGE = 96
MESH = pl.DeviceIdType.MESH


def filter_coefficients():
    return (
        (11.0 + 10.0 * ALPHA_F) / 16.0,
        (15.0 + 34.0 * ALPHA_F) / 32.0,
        (-3.0 + 6.0 * ALPHA_F) / 16.0,
        (1.0 - 2.0 * ALPHA_F) / 32.0,
    )


def line_kernel(alpha, stencil):
    root = np.sqrt(1.0 - 4.0 * alpha * alpha)
    rate = (-1.0 + root) / (2.0 * alpha)

    def response(n):
        n = np.asarray(n)
        return sum(s * rate ** np.abs(n + m) / root for m, s in stencil.items())

    far = max(stencil)
    return response, rate, float(response(far) / rate**far)


def slope_kernel():
    a, b = 0.5 * COEF_A, 0.25 * COEF_B
    response, rate, factor = line_kernel(ALPHA_D, {1: 0.5 * a, -1: -0.5 * a, 2: 0.5 * b, -2: -0.5 * b})
    return response, rate, factor, float(response(1)) - factor * rate


def smooth_kernel():
    c = filter_coefficients()
    stencil = {0: -c[0]}
    for n in (1, 2, 3):
        stencil[n] = stencil[-n] = -0.5 * c[n]
    response, rate, factor = line_kernel(ALPHA_F, stencil)
    near = [float(response(n)) - factor * rate**n for n in (1, 2)]
    return response, rate, factor, near


def halves(table):
    table = np.asarray(table, np.float32)
    high = table.astype(ml_dtypes.bfloat16)
    low = (table - high.astype(np.float32)).astype(ml_dtypes.bfloat16)
    return high, low


def tables():
    response, rate, factor, near = slope_kernel()
    i = np.arange(LX)
    k = np.arange(LZ)
    rows = np.zeros((LX + 16, LX))
    rows[:LX] = response(i[:, None] - i[None, :])
    rows[LX] = factor * rate ** (LX - i)
    rows[LX + 1] = -factor * rate ** (i + 1.0)
    slope_x = np.concatenate(halves(rows))
    high, low = halves(response(k[None, :] - k[:, None]))
    slope_z = np.block([[high, low], [high, np.zeros_like(low)]])
    sends = np.zeros((32, 6, LZ))
    for f in range(6):
        sends[f, f] = factor * rate ** (LZ - k)
        sends[6 + f, f, LZ - 1] = 1.0
        sends[16 + f, f] = -factor * rate ** (k + 1.0)
        sends[22 + f, f, 0] = 1.0
    high, low = halves(sends)
    none = np.zeros_like(low)
    send_z = np.concatenate(
        [np.concatenate([high, high], axis=2), np.concatenate([low, none], axis=2)]
    ).reshape(64, 6 * 2 * LZ)
    spread = np.zeros((32, 6, LZ))
    for f in range(6):
        spread[f, f] = rate**k
        spread[6 + f, f, 0] = near
        spread[16 + f, f] = rate ** (LZ - 1.0 - k)
        spread[22 + f, f, LZ - 1] = -near
    high, low = halves(spread.reshape(32, 6 * LZ))
    spread_z = np.concatenate([high, high, low])
    fade_x = np.zeros((2, EDGE, LZ), np.float32)
    fade_x[0] = (rate ** i[:EDGE])[:, None]
    fade_x[1] = fade_x[0, ::-1]
    response, rate, factor, _ = smooth_kernel()
    smooth_x = np.concatenate(halves(response(i[:, None] - i[None, :])))
    fade_f = np.zeros((2, LX, LZ), np.float32)
    fade_f[0] = (rate**i)[:, None]
    fade_f[1] = fade_f[0, ::-1]
    return send_z, slope_x, slope_z, spread_z, fade_x, fade_f, smooth_x


def split(values):
    high = values.astype(jnp.bfloat16)
    low = (values - high.astype(jnp.float32)).astype(jnp.bfloat16)
    return high, low


def dot(a, b, dims=((1,), (0,))):
    return lax.dot_general(a, b, (dims, ((), ())), preferred_element_type=jnp.float32)


def kernel(
    counts,
    velocity_hbm, send_z_hbm, slope_x_hbm, slope_z_hbm, spread_z_hbm, fade_x_hbm, fade_f_hbm, smooth_x_hbm,
    out,
    v, send_z, slope_x, slope_z, spread_z, fade_x, fade_f, smooth_x,
    fields, part_x, h, h_halves,
    z_out, z_in, x_out, x_in, f_out, f_in,
    load_sem, send_sem, recv_sem,
):
    nx, nz = counts
    gx, gz = lax.axis_index("gx"), lax.axis_index("gz")
    x_next, x_prev = lax.rem(gx + 1, nx), lax.rem(gx + nx - 1, nx)
    z_next, z_prev = lax.rem(gz + 1, nz), lax.rem(gz + nz - 1, nz)
    sides_z = ((gx, z_next), (gx, z_prev))
    sides_x = ((x_next, gz), (x_prev, gz))

    barrier = pltpu.get_barrier_semaphore()
    for side in sides_z + sides_x:
        pl.semaphore_signal(barrier, inc=1, device_id=side, device_id_type=MESH)

    loads = [
        pltpu.make_async_copy(src, dst, load_sem.at[n])
        for n, (src, dst) in enumerate(
            (
                (velocity_hbm, v),
                (send_z_hbm, send_z),
                (slope_x_hbm, slope_x),
                (slope_z_hbm, slope_z),
                (spread_z_hbm, spread_z),
                (fade_x_hbm, fade_x),
                (fade_f_hbm, fade_f),
                (smooth_x_hbm, smooth_x),
            )
        )
    ]
    for load in loads:
        load.start()

    loads[0].wait()
    u, w = v[0], v[2]
    for n, field in enumerate((u * u, u * v[1], u, v[1], w, u * w, w * v[1], w * w)):
        high, low = split(field)
        fields[:, n * 256 : n * 256 + 128] = high
        fields[:, n * 256 + 128 : n * 256 + 256] = low

    loads[1].wait()
    both = dot(send_z[...], fields[:, 512:], ((1,), (1,)))
    z_out[...] = both[:32] + both[32:]
    pl.semaphore_wait(barrier, 4)
    copies_z = []
    for n, side in enumerate(sides_z):
        copies_z.append(
            pltpu.make_async_remote_copy(
                src_ref=z_out.at[pl.ds(16 * n, 16)],
                dst_ref=z_in.at[pl.ds(16 * n, 16)],
                send_sem=send_sem.at[n],
                recv_sem=recv_sem.at[n],
                device_id=side,
                device_id_type=MESH,
            )
        )
        copies_z[-1].start()

    loads[2].wait()
    for f in range(6):
        full = dot(slope_x[...], fields[:, f * 256 : f * 256 + 256])
        part = full[: LX + 16, :128] + full[: LX + 16, 128:] + full[LX + 16 :, :128]
        part_x[f] = part[:LX]
        x_out[0, f : f + 1] = part[LX : LX + 1]
        x_out[1, f : f + 1] = part[LX + 1 : LX + 2]
    for side, row in ((0, LX - 1), (1, 0)):
        ur, vr, wr = v[0, row : row + 1], v[1, row : row + 1], v[2, row : row + 1]
        for f, value in enumerate((ur * ur, ur * vr, ur, vr, wr, ur * wr)):
            x_out[side, 6 + f : 7 + f] = value
    copies_x = []
    for n, side in enumerate(sides_x):
        copies_x.append(
            pltpu.make_async_remote_copy(
                src_ref=x_out.at[n],
                dst_ref=x_in.at[n],
                send_sem=send_sem.at[2 + n],
                recv_sem=recv_sem.at[2 + n],
                device_id=side,
                device_id_type=MESH,
            )
        )
        copies_x[-1].start()

    loads[3].wait()
    flat = (0, 1, 5)
    for c in range(3):
        total = part_x[flat[c]] + u * part_x[2 + c]
        for f, factor in ((2 + c, w), (5 + c, None)):
            full = dot(fields[:, f * 256 : f * 256 + 256], slope_z[...])
            part = full[:, :128] + full[:, 128:]
            total = total + (part if factor is None else factor * part)
        h[c] = total

    for load in loads[4:]:
        load.wait()
    _, _, _, near_d = slope_kernel()
    first = lax.broadcasted_iota(jnp.int32, (8, LZ), 0) == 0
    last = lax.broadcasted_iota(jnp.int32, (8, LZ), 0) == 7
    for copy in copies_x:
        copy.wait()
    for c in range(3):
        uv, vc = flat[c], 2 + c
        rows = slice(0, EDGE)
        h[c, rows] += fade_x[0] * (x_in[0, uv : uv + 1] + v[0, rows] * x_in[0, vc : vc + 1])
        near = x_in[0, 6 + uv : 7 + uv] + v[0, 0:8] * x_in[0, 6 + vc : 7 + vc]
        h[c, 0:8] += jnp.where(first, near_d * near, 0.0)
        rows = slice(LX - EDGE, LX)
        h[c, rows] += fade_x[1] * (x_in[1, uv : uv + 1] + v[0, rows] * x_in[1, vc : vc + 1])
        near = x_in[1, 6 + uv : 7 + uv] + v[0, LX - 8 : LX] * x_in[1, 6 + vc : 7 + vc]
        h[c, LX - 8 : LX] -= jnp.where(last, near_d * near, 0.0)

    for copy in copies_z:
        copy.wait()
    high, low = split(z_in[...])
    spread = dot(jnp.concatenate([high, low, high]), spread_z[...], ((0,), (0,)))
    for c in range(3):
        at, to = (3 + c) * 128, c * 128
        h[c] += spread[:, at : at + 128] + w * spread[:, to : to + 128]

    for c in range(3):
        for side, (a, b) in enumerate(((LX - 1, LX - 2), (0, 1))):
            f_out[side, c : c + 1] = jnp.sum(fade_f[1 - side] * h[c], axis=0, keepdims=True)
            f_out[side, 3 + c : 4 + c] = h[c, a : a + 1]
            f_out[side, 6 + c : 7 + c] = h[c, b : b + 1]
    copies_f = []
    for n, side in enumerate(sides_x):
        copies_f.append(
            pltpu.make_async_remote_copy(
                src_ref=f_out.at[n],
                dst_ref=f_in.at[n],
                send_sem=send_sem.at[4 + n],
                recv_sem=recv_sem.at[4 + n],
                device_id=side,
                device_id_type=MESH,
            )
        )
        copies_f[-1].start()

    for c in range(3):
        high, low = split(h[c])
        h_halves[c, :, :128] = high
        h_halves[c, :, 128:] = low
        full = dot(smooth_x[...], h_halves[c])
        out[c] = full[:LX, :128] + full[:LX, 128:] + full[LX:, :128]

    _, rate, factor, (near1, near2) = smooth_kernel()
    row = lax.broadcasted_iota(jnp.int32, (8, LZ), 0)
    for copy in copies_f:
        copy.wait()
    for c in range(3):
        scale = rate * factor
        below, above = scale * f_in[0, c : c + 1], scale * f_in[1, c : c + 1]
        out[c] += fade_f[0] * below + fade_f[1] * above
        for side, start, end0, end1 in ((0, 0, 0, 1), (1, LX - 8, 7, 6)):
            cell1, cell2 = f_in[side, 3 + c : 4 + c], f_in[side, 6 + c : 7 + c]
            out[c, start : start + 8] += jnp.where(row == end0, near1 * cell1 + near2 * cell2, 0.0) + jnp.where(
                row == end1, near2 * cell1, 0.0
            )


def per_device(counts, velocity):
    operands = [pltpu.with_memory_space_constraint(jnp.asarray(t), pltpu.HBM) for t in tables()]
    bf16, f32 = jnp.bfloat16, jnp.float32
    flat = pltpu.with_memory_space_constraint(velocity.reshape(3, LX, LZ), pltpu.HBM)
    out = pl.pallas_call(
        lambda *refs: kernel(counts, *refs),
        out_shape=jax.ShapeDtypeStruct((3, LX, LZ), f32),
        in_specs=[pl.BlockSpec(memory_space=pltpu.HBM)] * 8,
        out_specs=pl.BlockSpec(memory_space=pltpu.VMEM),
        scratch_shapes=[pltpu.VMEM((3, LX, LZ), f32)]
        + [pltpu.VMEM(t.shape, t.dtype) for t in operands]
        + [
            pltpu.VMEM((LX, 8 * 256), bf16),
            pltpu.VMEM((6, LX, LZ), f32),
            pltpu.VMEM((3, LX, LZ), f32),
            pltpu.VMEM((3, LX, 2 * LZ), bf16),
            pltpu.VMEM((32, LX), f32),
            pltpu.VMEM((32, LX), f32),
            pltpu.VMEM((2, 16, LZ), f32),
            pltpu.VMEM((2, 16, LZ), f32),
            pltpu.VMEM((2, 16, LZ), f32),
            pltpu.VMEM((2, 16, LZ), f32),
            pltpu.SemaphoreType.DMA((8,)),
            pltpu.SemaphoreType.DMA((6,)),
            pltpu.SemaphoreType.DMA((6,)),
        ],
        compiler_params=pltpu.CompilerParams(collective_id=0, has_side_effects=True, vmem_limit_bytes=32 * 2**20),
    )(flat, *operands)
    return out.reshape(3, LX, 1, LZ)


def solution(mesh):
    counts = (mesh.shape["gx"], mesh.shape["gz"])
    return jax.shard_map(
        lambda velocity: per_device(counts, velocity),
        mesh=mesh,
        in_specs=(P(None, "gx", None, "gz"),),
        out_specs=P(None, "gx", None, "gz"),
        check_vma=False,
    )
```

```python
import jax
import jax.numpy as jnp
import ml_dtypes
import numpy as np
from jax import lax
from jax.experimental import pallas as pl
from jax.experimental.pallas import tpu as pltpu
from jax.sharding import PartitionSpec as P

ALPHA_D = 1.0 / 3.0
COEF_A = 14.0 / 9.0
COEF_B = 1.0 / 9.0
ALPHA_F = 0.49
LX = 256
LZ = 128
EDGE = 96
EARLY = 3
MESH = pl.DeviceIdType.MESH


def filter_coefficients():
    return (
        (11.0 + 10.0 * ALPHA_F) / 16.0,
        (15.0 + 34.0 * ALPHA_F) / 32.0,
        (-3.0 + 6.0 * ALPHA_F) / 16.0,
        (1.0 - 2.0 * ALPHA_F) / 32.0,
    )


def line_kernel(alpha, stencil):
    root = np.sqrt(1.0 - 4.0 * alpha * alpha)
    rate = (-1.0 + root) / (2.0 * alpha)

    def response(n):
        n = np.asarray(n)
        return sum(s * rate ** np.abs(n + m) / root for m, s in stencil.items())

    far = max(stencil)
    return response, rate, float(response(far) / rate**far)


def slope_kernel():
    a, b = 0.5 * COEF_A, 0.25 * COEF_B
    response, rate, factor = line_kernel(ALPHA_D, {1: 0.5 * a, -1: -0.5 * a, 2: 0.5 * b, -2: -0.5 * b})
    return response, rate, factor, float(response(1)) - factor * rate


def smooth_kernel():
    c = filter_coefficients()
    stencil = {0: -c[0]}
    for n in (1, 2, 3):
        stencil[n] = stencil[-n] = -0.5 * c[n]
    response, rate, factor = line_kernel(ALPHA_F, stencil)
    near = [float(response(n)) - factor * rate**n for n in (1, 2)]
    return response, rate, factor, near


def halves(table):
    table = np.asarray(table, np.float32)
    high = table.astype(ml_dtypes.bfloat16)
    low = (table - high.astype(np.float32)).astype(ml_dtypes.bfloat16)
    return high, low


def tables():
    response, rate, factor, near = slope_kernel()
    i = np.arange(LX)
    k = np.arange(LZ)
    slope_x = np.concatenate(halves(response(i[:, None] - i[None, :])))
    high, low = halves(response(k[None, :] - k[:, None]))
    slope_z = np.block([[high, low], [high, np.zeros_like(low)]])
    sends = np.zeros((8, LZ))
    sends[0] = factor * rate ** (LZ - k)
    sends[1, LZ - 1] = 1.0
    sends[2] = -factor * rate ** (k + 1.0)
    sends[3, 0] = 1.0
    high, low = halves(sends)
    send_z = np.block([[high, high], [low, np.zeros_like(low)]])
    spread = np.zeros((32, 6, LZ))
    for f in range(6):
        spread[2 * f, f] = rate**k
        spread[2 * f + 1, f, 0] = near
        spread[16 + 2 * f, f] = rate ** (LZ - 1.0 - k)
        spread[17 + 2 * f, f, LZ - 1] = -near
    high, low = halves(spread.reshape(32, 6 * LZ))
    spread_z = np.concatenate([high, high, low])
    fade_x = np.zeros((2, EDGE, LZ), np.float32)
    fade_x[0] = (rate ** i[:EDGE])[:, None]
    fade_x[1] = fade_x[0, ::-1]
    response, rate, factor, _ = smooth_kernel()
    smooth_x = np.concatenate(halves(response(i[:, None] - i[None, :])))
    fade_f = np.zeros((2, LX, LZ), np.float32)
    fade_f[0] = (rate**i)[:, None]
    fade_f[1] = fade_f[0, ::-1]
    return fade_x, send_z, slope_x, slope_z, spread_z, fade_f, smooth_x


def split(values):
    high = values.astype(jnp.bfloat16)
    low = (values - high.astype(jnp.float32)).astype(jnp.bfloat16)
    return high, low


def dot(a, b, dims=((1,), (0,))):
    return lax.dot_general(a, b, (dims, ((), ())), preferred_element_type=jnp.float32)


def total(values):
    return jnp.sum(values, axis=0, keepdims=True)


def kernel(
    counts,
    velocity_hbm, fade_x_hbm, send_z_hbm, slope_x_hbm, slope_z_hbm, spread_z_hbm, fade_f_hbm, smooth_x_hbm,
    out,
    v, fade_x, send_z, slope_x, slope_z, spread_z, fade_f, smooth_x,
    fields, part_x, h, h_halves,
    z_out, z_in, x_out, x_in, f_out, f_in,
    load_sem, send_sem, recv_sem, ready,
):
    nx, nz = counts
    gx, gz = lax.axis_index("gx"), lax.axis_index("gz")
    x_next, x_prev = lax.rem(gx + 1, nx), lax.rem(gx + nx - 1, nx)
    z_next, z_prev = lax.rem(gz + 1, nz), lax.rem(gz + nz - 1, nz)
    sides_z = ((gx, z_next), (gx, z_prev))
    sides_x = ((x_next, gz), (x_prev, gz))
    is_first, is_last = gx == 0, gx == nx - 1

    def signal(semaphore, side):
        pl.semaphore_signal(semaphore, inc=1, device_id=side, device_id_type=MESH)

    def remote(source, target, n, side):
        return pltpu.make_async_remote_copy(
            src_ref=source,
            dst_ref=target,
            send_sem=send_sem.at[n],
            recv_sem=recv_sem.at[n],
            device_id=side,
            device_id_type=MESH,
        )

    loads = [
        pltpu.make_async_copy(src, dst, load_sem.at[n])
        for n, (src, dst) in enumerate(
            (
                (velocity_hbm, v),
                (fade_x_hbm, fade_x),
                (send_z_hbm, send_z),
                (slope_x_hbm, slope_x),
                (slope_z_hbm, slope_z),
                (spread_z_hbm, spread_z),
                (fade_f_hbm, fade_f),
                (smooth_x_hbm, smooth_x),
            )
        )
    ]
    for load in loads[:EARLY]:
        load.start()

    barrier = pltpu.get_barrier_semaphore()
    for side in sides_z + (sides_x[1],):
        signal(barrier, side)

    @pl.when(jnp.logical_not(is_last))
    def _():
        signal(barrier, sides_x[0])

    z_out[...] = jnp.zeros_like(z_out)
    for load in loads[:3]:
        load.wait()
    for load in loads[EARLY:]:
        load.start()
    u, w = v[0], v[2]
    values = (u * u, u * v[1], u, v[1], w, u * w, w * v[1], w * w)
    for n in (2, 3, 4, 5, 6, 7, 0, 1):
        high, low = split(values[n])
        fields[:, n * 256 : n * 256 + 128] = high
        fields[:, n * 256 + 128 : n * 256 + 256] = low

    for f in range(6):
        both = dot(send_z[...], fields[:, (2 + f) * 256 : (3 + f) * 256], ((1,), (1,)))
        both = both[:8] + both[8:]
        z_out[2 * f : 2 * f + 2] = both[0:2]
        z_out[16 + 2 * f : 18 + 2 * f] = both[2:4]

    rate_d, factor_d, near_d = slope_kernel()[1:]
    for side, row in ((0, LX - 1), (1, 0)):
        rows = slice(LX - EDGE, LX) if side == 0 else slice(0, EDGE)
        scale = factor_d * rate_d if side == 0 else -factor_d * rate_d
        for f in range(6):
            x_out[side, f : f + 1] = scale * total(fade_x[1 - side] * values[f][rows])
            x_out[side, 6 + f : 7 + f] = values[f][row : row + 1]

    pl.semaphore_wait(barrier, jnp.where(is_first, 3, 4))
    copies = [remote(z_out.at[pl.ds(16 * n, 16)], z_in.at[pl.ds(16 * n, 16)], n, sides_z[n]) for n in (0, 1)]
    copies += [remote(x_out.at[n], x_in.at[n], 2 + n, sides_x[n]) for n in (0, 1)]
    copies += [remote(f_out.at[n], f_in.at[n], 4 + n, sides_x[n]) for n in (0, 1)]
    for n in (0, 1, 2):
        copies[n].start()

    @pl.when(is_last)
    def _():
        signal(ready, sides_x[0])

    @pl.when(jnp.logical_not(is_first))
    def _():
        copies[3].start()

    loads[3].wait()
    loads[4].wait()
    flat = (0, 1, 5)
    for f in range(6):
        full = dot(slope_x[...], fields[:, f * 256 : f * 256 + 256])
        part_x[f] = full[:LX, :128] + full[:LX, 128:] + full[LX:, :128]
    for c in range(3):
        value = part_x[flat[c]] + v[0] * part_x[2 + c]
        for f, by_w in ((2 + c, True), (5 + c, False)):
            full = dot(fields[:, f * 256 : f * 256 + 256], slope_z[...])
            part = full[:, :128] + full[:, 128:]
            value = value + (v[2] * part if by_w else part)
        h[c] = value

    for load in loads[5:]:
        load.wait()

    top, end = slice(0, EDGE), slice(LX - EDGE, LX)
    f_out[0, 9:10] = total(fade_f[1, end] * (fade_x[1] * v[0, end]))
    f_out[0, 10:11] = v[0, LX - 1 : LX]
    f_out[0, 11:12] = v[0, LX - 2 : LX - 1]
    f_out[1, 9:10] = total(fade_f[0, top] * (fade_x[0] * v[0, top]))
    f_out[1, 10:11] = v[0, 0:1]
    f_out[1, 11:12] = v[0, 1:2]
    far = (
        total(fade_f[1, top] * (fade_x[0] * v[0, top])),
        total(fade_f[0, end] * (fade_x[1] * v[0, end])),
    )
    rate_f, factor_f, (near1, near2) = smooth_kernel()[1:]
    powers = np.arange(EDGE, dtype=np.float64)
    near_sum = float(np.sum((rate_f * rate_d) ** powers))
    far_sum = float(np.sum(rate_f ** (LX - 1 - powers) * rate_d**powers))
    far_end = float(rate_f ** (LX - 1))

    @pl.when(is_first)
    def _():
        pl.semaphore_wait(ready, 1)
        copies[3].start()

    copies[0].wait_recv()
    copies[1].wait_recv()
    high, low = split(z_in[...])
    spread = dot(jnp.concatenate([high, low, high]), spread_z[...], ((0,), (0,)))
    ends = []
    for c in range(3):
        at, to = (3 + c) * 128, c * 128
        value = h[c] + (spread[:, at : at + 128] + v[2] * spread[:, to : to + 128])
        h[c] = value
        ends.append((total(fade_f[1] * value), total(fade_f[0] * value)))

    first = lax.broadcasted_iota(jnp.int32, (8, LZ), 0) == 0
    last = lax.broadcasted_iota(jnp.int32, (8, LZ), 0) == 7
    for side, (edge, row0, row1) in enumerate(((0, LX - 1, LX - 2), (LX - 1, 0, 1))):
        copies[2 + side].wait_recv()
        sign = near_d if side == 0 else -near_d
        for c in range(3):
            uv, vc = flat[c], 2 + c
            from_far = far_sum * x_in[side, uv : uv + 1] + far[side] * x_in[side, vc : vc + 1]
            cell = x_in[side, 6 + uv : 7 + uv] + v[0, edge : edge + 1] * x_in[side, 6 + vc : 7 + vc]
            f_out[side, c : c + 1] = ends[c][side] + from_far + (sign * far_end) * cell
            f_out[side, 3 + c : 4 + c] = h[c, row0 : row0 + 1]
            f_out[side, 6 + c : 7 + c] = h[c, row1 : row1 + 1]
        copies[4 + side].start()

    for c in range(3):
        uv, vc = flat[c], 2 + c
        h[c, top] += fade_x[0] * (x_in[0, uv : uv + 1] + v[0, top] * x_in[0, vc : vc + 1])
        cell = x_in[0, 6 + uv : 7 + uv] + v[0, 0:8] * x_in[0, 6 + vc : 7 + vc]
        h[c, 0:8] += jnp.where(first, near_d * cell, 0.0)
        h[c, end] += fade_x[1] * (x_in[1, uv : uv + 1] + v[0, end] * x_in[1, vc : vc + 1])
        cell = x_in[1, 6 + uv : 7 + uv] + v[0, LX - 8 : LX] * x_in[1, 6 + vc : 7 + vc]
        h[c, LX - 8 : LX] -= jnp.where(last, near_d * cell, 0.0)

    for c in range(3):
        high, low = split(h[c])
        h_halves[c, :, :128] = high
        h_halves[c, :, 128:] = low
        full = dot(smooth_x[...], h_halves[c])
        out[c] = full[:LX, :128] + full[:LX, 128:] + full[LX:, :128]

    row = lax.broadcasted_iota(jnp.int32, (8, LZ), 0)
    copies[5].wait_recv()
    copies[4].wait_recv()
    scale = rate_f * factor_f
    for c in range(3):
        uv, vc = flat[c], 2 + c
        sums = []
        for side, sign, start, end0, end1 in ((0, -near_d, 0, 0, 1), (1, near_d, LX - 8, 7, 6)):
            own, own_v = x_out[1 - side, uv : uv + 1], x_out[1 - side, vc : vc + 1]
            edge, edge_v = x_out[1 - side, 6 + uv : 7 + uv], x_out[1 - side, 6 + vc : 7 + vc]
            moment, u1, u2 = (f_in[side, n : n + 1] for n in (9, 10, 11))
            cell = sign * (edge + u1 * edge_v)
            sums.append(scale * (f_in[side, c : c + 1] + near_sum * own + moment * own_v + cell))
            cell1 = f_in[side, 3 + c : 4 + c] + own + u1 * own_v + cell
            cell2 = f_in[side, 6 + c : 7 + c] + rate_d * (own + u2 * own_v)
            out[c, start : start + 8] += jnp.where(row == end0, near1 * cell1 + near2 * cell2, 0.0) + jnp.where(
                row == end1, near2 * cell1, 0.0
            )
        out[c] += fade_f[0] * sums[0] + fade_f[1] * sums[1]
    for copy in copies:
        copy.wait_send()


def per_device(counts, velocity):
    operands = [pltpu.with_memory_space_constraint(jnp.asarray(t), pltpu.HBM) for t in tables()]
    bf16, f32 = jnp.bfloat16, jnp.float32
    flat = pltpu.with_memory_space_constraint(velocity.reshape(3, LX, LZ), pltpu.HBM)
    out = pl.pallas_call(
        lambda *refs: kernel(counts, *refs),
        out_shape=jax.ShapeDtypeStruct((3, LX, LZ), f32),
        in_specs=[pl.BlockSpec(memory_space=pltpu.HBM)] * 8,
        out_specs=pl.BlockSpec(memory_space=pltpu.VMEM),
        scratch_shapes=[pltpu.VMEM((3, LX, LZ), f32)]
        + [pltpu.VMEM(t.shape, t.dtype) for t in operands]
        + [
            pltpu.VMEM((LX, 8 * 256), bf16),
            pltpu.VMEM((6, LX, LZ), f32),
            pltpu.VMEM((3, LX, LZ), f32),
            pltpu.VMEM((3, LX, 2 * LZ), bf16),
            pltpu.VMEM((32, LX), f32),
            pltpu.VMEM((32, LX), f32),
            pltpu.VMEM((2, 16, LZ), f32),
            pltpu.VMEM((2, 16, LZ), f32),
            pltpu.VMEM((2, 16, LZ), f32),
            pltpu.VMEM((2, 16, LZ), f32),
            pltpu.SemaphoreType.DMA((8,)),
            pltpu.SemaphoreType.DMA((6,)),
            pltpu.SemaphoreType.DMA((6,)),
            pltpu.SemaphoreType.REGULAR,
        ],
        compiler_params=pltpu.CompilerParams(collective_id=0, has_side_effects=True, vmem_limit_bytes=32 * 2**20),
    )(flat, *operands)
    return out.reshape(3, LX, 1, LZ)


def solution(mesh):
    counts = (mesh.shape["gx"], mesh.shape["gz"])
    return jax.shard_map(
        lambda velocity: per_device(counts, velocity),
        mesh=mesh,
        in_specs=(P(None, "gx", None, "gz"),),
        out_specs=P(None, "gx", None, "gz"),
        check_vma=False,
    )
```

```python
import jax
import jax.numpy as jnp
import ml_dtypes
import numpy as np
from jax import lax
from jax.experimental import pallas as pl
from jax.experimental.pallas import tpu as pltpu
from jax.sharding import PartitionSpec as P

ALPHA_D = 1.0 / 3.0
COEF_A = 14.0 / 9.0
COEF_B = 1.0 / 9.0
ALPHA_F = 0.49
LX = 256
LZ = 128
EDGE = 96
EARLY = 3
SEAM = 8
MESH = pl.DeviceIdType.MESH


def filter_coefficients():
    return (
        (11.0 + 10.0 * ALPHA_F) / 16.0,
        (15.0 + 34.0 * ALPHA_F) / 32.0,
        (-3.0 + 6.0 * ALPHA_F) / 16.0,
        (1.0 - 2.0 * ALPHA_F) / 32.0,
    )


def line_kernel(alpha, stencil):
    root = np.sqrt(1.0 - 4.0 * alpha * alpha)
    rate = (-1.0 + root) / (2.0 * alpha)

    def response(n):
        n = np.asarray(n)
        return sum(s * rate ** np.abs(n + m) / root for m, s in stencil.items())

    far = max(stencil)
    return response, rate, float(response(far) / rate**far)


def slope_kernel():
    a, b = 0.5 * COEF_A, 0.25 * COEF_B
    response, rate, factor = line_kernel(ALPHA_D, {1: 0.5 * a, -1: -0.5 * a, 2: 0.5 * b, -2: -0.5 * b})
    return response, rate, factor, float(response(1)) - factor * rate


def smooth_kernel():
    c = filter_coefficients()
    stencil = {0: -c[0]}
    for n in (1, 2, 3):
        stencil[n] = stencil[-n] = -0.5 * c[n]
    response, rate, factor = line_kernel(ALPHA_F, stencil)
    near = [float(response(n)) - factor * rate**n for n in (1, 2)]
    return response, rate, factor, near


def halves(table):
    table = np.asarray(table, np.float32)
    high = table.astype(ml_dtypes.bfloat16)
    low = (table - high.astype(np.float32)).astype(ml_dtypes.bfloat16)
    return high, low


def tables():
    response, rate, factor, near = slope_kernel()
    i = np.arange(LX)
    k = np.arange(LZ)
    slope_x = np.concatenate(halves(response(i[:, None] - i[None, :])))
    high, low = halves(response(k[None, :] - k[:, None]))
    slope_z = np.block([[high, low], [high, np.zeros_like(low)]])
    sends = np.zeros((8, LZ))
    sends[0] = factor * rate ** (LZ - k)
    sends[1, LZ - 1] = 1.0
    sends[2] = -factor * rate ** (k + 1.0)
    sends[3, 0] = 1.0
    high, low = halves(sends)
    send_z = np.block([[high, high], [low, np.zeros_like(low)]])
    spread = np.zeros((32, 6, LZ))
    for f in range(6):
        spread[2 * f, f] = rate**k
        spread[2 * f + 1, f, 0] = near
        spread[16 + 2 * f, f] = rate ** (LZ - 1.0 - k)
        spread[17 + 2 * f, f, LZ - 1] = -near
    high, low = halves(spread.reshape(32, 6 * LZ))
    spread_z = np.concatenate([high, high, low])
    fade_x = np.zeros((2, EDGE, LZ), np.float32)
    fade_x[0] = (rate ** i[:EDGE])[:, None]
    fade_x[1] = fade_x[0, ::-1]
    response, rate, factor, _ = smooth_kernel()
    smooth_x = np.concatenate(halves(response(i[:, None] - i[None, :])))
    fade_f = np.zeros((2, LX, LZ), np.float32)
    fade_f[0] = (rate**i)[:, None]
    fade_f[1] = fade_f[0, ::-1]
    return fade_x, send_z, slope_x, slope_z, spread_z, fade_f, smooth_x


def split(values):
    high = values.astype(jnp.bfloat16)
    low = (values - high.astype(jnp.float32)).astype(jnp.bfloat16)
    return high, low


def dot(a, b, dims=((1,), (0,))):
    return lax.dot_general(a, b, (dims, ((), ())), preferred_element_type=jnp.float32)


def total(values):
    return jnp.sum(values, axis=0, keepdims=True)


def kernel(
    counts,
    velocity_hbm, fade_x_hbm, send_z_hbm, slope_x_hbm, slope_z_hbm, spread_z_hbm, fade_f_hbm, smooth_x_hbm,
    out,
    v, fade_x, send_z, slope_x, slope_z, spread_z, fade_f, smooth_x,
    fields, part_x, h, h_halves,
    z_out, z_in, z_use, z_far, w_far, x_out, x_in, f_out, f_in, ends, extra,
    load_sem, send_sem, recv_sem, ready, token,
):
    nx, nz = counts
    gx, gz = lax.axis_index("gx"), lax.axis_index("gz")
    x_next, x_prev = lax.rem(gx + 1, nx), lax.rem(gx + nx - 1, nx)
    z_next, z_prev = lax.rem(gz + 1, nz), lax.rem(gz + nz - 1, nz)
    sides_z = ((gx, z_next), (gx, z_prev))
    sides_x = ((x_next, gz), (x_prev, gz))
    is_first, is_last = gx == 0, gx == nx - 1
    ahead, behind = lax.rem(gz, SEAM) == SEAM - 1, lax.rem(gz, SEAM) == 0
    last_ahead, last_behind = jnp.logical_and(is_last, ahead), jnp.logical_and(is_last, behind)
    last_seam = jnp.logical_or(last_ahead, last_behind)
    first_seam = jnp.logical_and(is_first, jnp.logical_or(ahead, behind))

    def signal(semaphore, side):
        pl.semaphore_signal(semaphore, inc=1, device_id=side, device_id_type=MESH)

    def remote(source, target, n, side):
        return pltpu.make_async_remote_copy(
            src_ref=source,
            dst_ref=target,
            send_sem=send_sem.at[n],
            recv_sem=recv_sem.at[n],
            device_id=side,
            device_id_type=MESH,
        )

    loads = [
        pltpu.make_async_copy(src, dst, load_sem.at[n])
        for n, (src, dst) in enumerate(
            (
                (velocity_hbm, v),
                (fade_x_hbm, fade_x),
                (send_z_hbm, send_z),
                (slope_x_hbm, slope_x),
                (slope_z_hbm, slope_z),
                (spread_z_hbm, spread_z),
                (fade_f_hbm, fade_f),
                (smooth_x_hbm, smooth_x),
            )
        )
    ]
    for load in loads[:EARLY]:
        load.start()

    z_use[...] = jnp.zeros_like(z_use)
    z_far[...] = jnp.zeros_like(z_far)
    extra[...] = jnp.zeros_like(extra)
    barrier = pltpu.get_barrier_semaphore()
    signal(barrier, sides_z[1])

    @pl.when(jnp.logical_not(last_ahead))
    def _():
        signal(barrier, sides_z[0])

    @pl.when(jnp.logical_not(is_first))
    def _():
        signal(barrier, sides_x[1])

    @pl.when(jnp.logical_not(is_last))
    def _():
        signal(barrier, sides_x[0])

    z_out[...] = jnp.zeros_like(z_out)
    for load in loads[:3]:
        load.wait()
    for load in loads[EARLY:]:
        load.start()
    u, w = v[0], v[2]
    values = (u * u, u * v[1], u, v[1], w, u * w, w * v[1], w * w)
    for n in (2, 3, 4, 5, 6, 7, 0, 1):
        high, low = split(values[n])
        fields[:, n * 256 : n * 256 + 128] = high
        fields[:, n * 256 + 128 : n * 256 + 256] = low

    for f in range(6):
        both = dot(send_z[...], fields[:, (2 + f) * 256 : (3 + f) * 256], ((1,), (1,)))
        both = both[:8] + both[8:]
        z_out[2 * f : 2 * f + 2] = both[0:2]
        z_out[16 + 2 * f : 18 + 2 * f] = both[2:4]

    rate_d, factor_d, near_d = slope_kernel()[1:]
    for side, row in ((0, LX - 1), (1, 0)):
        rows = slice(LX - EDGE, LX) if side == 0 else slice(0, EDGE)
        scale = factor_d * rate_d if side == 0 else -factor_d * rate_d
        for f in range(6):
            x_out[side, f : f + 1] = scale * total(fade_x[1 - side] * values[f][rows])
            x_out[side, 6 + f : 7 + f] = values[f][row : row + 1]

    pl.semaphore_wait(barrier, jnp.where(jnp.logical_or(is_first, last_behind), 3, 4))

    @pl.when(last_ahead)
    def _():
        signal(token, sides_z[0])

    @pl.when(is_last)
    def _():
        signal(ready, sides_x[0])

    @pl.when(is_first)
    def _():
        signal(barrier, sides_x[1])

    halves_z = [pl.ds(16 * n, 16) for n in (0, 1)]
    copies = [remote(z_out.at[halves_z[n]], z_in.at[halves_z[n]], n, sides_z[n]) for n in (0, 1)]
    copies += [remote(x_out.at[n], x_in.at[n], 2 + n, sides_x[n]) for n in (0, 1)]
    copies += [remote(f_out.at[n], f_in.at[n], 4 + n, sides_x[n]) for n in (0, 1)]
    far = [remote(z_out.at[halves_z[n]], z_far.at[halves_z[n]], 6, (x_next, sides_z[n][1])) for n in (0, 1)]
    far_w = remote(v.at[2], w_far, 7, sides_x[0])
    copies[0].start()

    @pl.when(jnp.logical_not(last_behind))
    def _():
        copies[1].start()

    @pl.when(last_ahead)
    def _():
        far[0].start()

    @pl.when(last_behind)
    def _():
        far[1].start()

    copies[2].start()

    @pl.when(jnp.logical_not(is_first))
    def _():
        copies[3].start()

    @pl.when(last_seam)
    def _():
        far_w.start()

    loads[3].wait()
    loads[4].wait()
    flat = (0, 1, 5)
    for f in range(6):
        full = dot(slope_x[...], fields[:, f * 256 : f * 256 + 256])
        part_x[f] = full[:LX, :128] + full[:LX, 128:] + full[LX:, :128]
    for c in range(3):
        value = part_x[flat[c]] + v[0] * part_x[2 + c]
        for f, by_w in ((2 + c, True), (5 + c, False)):
            full = dot(fields[:, f * 256 : f * 256 + 256], slope_z[...])
            part = full[:, :128] + full[:, 128:]
            value = value + (v[2] * part if by_w else part)
        h[c] = value

    for load in loads[5:]:
        load.wait()

    top, end = slice(0, EDGE), slice(LX - EDGE, LX)
    f_out[0, 9:10] = total(fade_f[1, end] * (fade_x[1] * v[0, end]))
    f_out[0, 10:11] = v[0, LX - 1 : LX]
    f_out[0, 11:12] = v[0, LX - 2 : LX - 1]
    f_out[1, 9:10] = total(fade_f[0, top] * (fade_x[0] * v[0, top]))
    f_out[1, 10:11] = v[0, 0:1]
    f_out[1, 11:12] = v[0, 1:2]
    moments = (
        total(fade_f[1, top] * (fade_x[0] * v[0, top])),
        total(fade_f[0, end] * (fade_x[1] * v[0, end])),
    )
    rate_f, factor_f, (near1, near2) = smooth_kernel()[1:]
    powers = np.arange(EDGE, dtype=np.float64)
    near_sum = float(np.sum((rate_f * rate_d) ** powers))
    far_sum = float(np.sum(rate_f ** (LX - 1 - powers) * rate_d**powers))
    far_end = float(rate_f ** (LX - 1))

    def spread_of(sums, w_cells):
        high, low = split(sums)
        spread = dot(jnp.concatenate([high, low, high]), spread_z[...], ((0,), (0,)))
        return [spread[:, n * 128 + 384 : n * 128 + 512] + w_cells * spread[:, n * 128 : n * 128 + 128] for n in range(3)]

    @pl.when(jnp.logical_not(last_behind))
    def _():
        copies[0].wait_recv()
        z_use[0:16] = z_in[0:16]

    @pl.when(jnp.logical_not(last_ahead))
    def _():
        copies[1].wait_recv()
        z_use[16:32] = z_in[16:32]

    for c, part in enumerate(spread_of(z_use[...], v[2])):
        value = h[c] + part
        h[c] = value
        ends[0, c : c + 1] = total(fade_f[1] * value)
        ends[1, c : c + 1] = total(fade_f[0] * value)

    first = lax.broadcasted_iota(jnp.int32, (8, LZ), 0) == 0
    last = lax.broadcasted_iota(jnp.int32, (8, LZ), 0) == 7
    for side, (edge, row0, row1) in enumerate(((0, LX - 1, LX - 2), (LX - 1, 0, 1))):
        if side == 1:

            @pl.when(is_first)
            def _():
                pl.semaphore_wait(ready, 1)
                copies[3].start()

            @pl.when(last_behind)
            def _():
                pl.semaphore_wait(token, 1)
                copies[1].start()
                copies[0].wait_recv()
                z_use[0:16] = z_in[0:16]
                z_use[16:32] = jnp.zeros_like(z_use[16:32])

            @pl.when(last_ahead)
            def _():
                copies[1].wait_recv()
                z_use[16:32] = z_in[16:32]
                z_use[0:16] = jnp.zeros_like(z_use[0:16])

            @pl.when(last_seam)
            def _():
                for c, part in enumerate(spread_of(z_use[...], v[2])):
                    value = h[c] + part
                    h[c] = value
                    ends[1, c : c + 1] = total(fade_f[0] * value)

        copies[2 + side].wait_recv()
        sign = near_d if side == 0 else -near_d
        for c in range(3):
            uv, vc = flat[c], 2 + c
            from_far = far_sum * x_in[side, uv : uv + 1] + moments[side] * x_in[side, vc : vc + 1]
            cell = x_in[side, 6 + uv : 7 + uv] + v[0, edge : edge + 1] * x_in[side, 6 + vc : 7 + vc]
            f_out[side, c : c + 1] = ends[side, c : c + 1] + from_far + (sign * far_end) * cell
            f_out[side, 3 + c : 4 + c] = h[c, row0 : row0 + 1]
            f_out[side, 6 + c : 7 + c] = h[c, row1 : row1 + 1]
        copies[4 + side].start()

    for c in range(3):
        uv, vc = flat[c], 2 + c
        h[c, top] += fade_x[0] * (x_in[0, uv : uv + 1] + v[0, top] * x_in[0, vc : vc + 1])
        cell = x_in[0, 6 + uv : 7 + uv] + v[0, 0:8] * x_in[0, 6 + vc : 7 + vc]
        h[c, 0:8] += jnp.where(first, near_d * cell, 0.0)
        h[c, end] += fade_x[1] * (x_in[1, uv : uv + 1] + v[0, end] * x_in[1, vc : vc + 1])
        cell = x_in[1, 6 + uv : 7 + uv] + v[0, LX - 8 : LX] * x_in[1, 6 + vc : 7 + vc]
        h[c, LX - 8 : LX] -= jnp.where(last, near_d * cell, 0.0)

    for c in range(3):
        high, low = split(h[c])
        h_halves[c, :, :128] = high
        h_halves[c, :, 128:] = low
        full = dot(smooth_x[...], h_halves[c])
        out[c] = full[:LX, :128] + full[:LX, 128:] + full[LX:, :128]

    @pl.when(first_seam)
    def _():
        far[0].wait_recv()
        far_w.wait_recv()
        for c, part in enumerate(spread_of(z_far[...], w_far[...])):
            extra[c : c + 1] = total(fade_f[1] * part)
            extra[3 + c : 4 + c] = part[LX - 1 : LX]
            extra[6 + c : 7 + c] = part[LX - 2 : LX - 1]

    row = lax.broadcasted_iota(jnp.int32, (8, LZ), 0)
    copies[5].wait_recv()
    copies[4].wait_recv()
    scale = rate_f * factor_f
    for c in range(3):
        uv, vc = flat[c], 2 + c
        sums = []
        for side, sign, start, end0, end1 in ((0, -near_d, 0, 0, 1), (1, near_d, LX - 8, 7, 6)):
            own, own_v = x_out[1 - side, uv : uv + 1], x_out[1 - side, vc : vc + 1]
            edge, edge_v = x_out[1 - side, 6 + uv : 7 + uv], x_out[1 - side, 6 + vc : 7 + vc]
            moment, u1, u2 = (f_in[side, n : n + 1] for n in (9, 10, 11))
            sent = [f_in[side, n : n + 1] + (extra[n : n + 1] if side == 0 else 0.0) for n in (c, 3 + c, 6 + c)]
            cell = sign * (edge + u1 * edge_v)
            sums.append(scale * (sent[0] + near_sum * own + moment * own_v + cell))
            cell1 = sent[1] + own + u1 * own_v + cell
            cell2 = sent[2] + rate_d * (own + u2 * own_v)
            out[c, start : start + 8] += jnp.where(row == end0, near1 * cell1 + near2 * cell2, 0.0) + jnp.where(
                row == end1, near2 * cell1, 0.0
            )
        out[c] += fade_f[0] * sums[0] + fade_f[1] * sums[1]
    for copy in copies:
        copy.wait_send()

    @pl.when(last_seam)
    def _():
        far[0].wait_send()
        far_w.wait_send()


def per_device(counts, velocity):
    operands = [pltpu.with_memory_space_constraint(jnp.asarray(t), pltpu.HBM) for t in tables()]
    bf16, f32 = jnp.bfloat16, jnp.float32
    flat = pltpu.with_memory_space_constraint(velocity.reshape(3, LX, LZ), pltpu.HBM)
    out = pl.pallas_call(
        lambda *refs: kernel(counts, *refs),
        out_shape=jax.ShapeDtypeStruct((3, LX, LZ), f32),
        in_specs=[pl.BlockSpec(memory_space=pltpu.HBM)] * 8,
        out_specs=pl.BlockSpec(memory_space=pltpu.VMEM),
        scratch_shapes=[pltpu.VMEM((3, LX, LZ), f32)]
        + [pltpu.VMEM(t.shape, t.dtype) for t in operands]
        + [
            pltpu.VMEM((LX, 8 * 256), bf16),
            pltpu.VMEM((6, LX, LZ), f32),
            pltpu.VMEM((3, LX, LZ), f32),
            pltpu.VMEM((3, LX, 2 * LZ), bf16),
            pltpu.VMEM((32, LX), f32),
            pltpu.VMEM((32, LX), f32),
            pltpu.VMEM((32, LX), f32),
            pltpu.VMEM((32, LX), f32),
            pltpu.VMEM((LX, LZ), f32),
            pltpu.VMEM((2, 16, LZ), f32),
            pltpu.VMEM((2, 16, LZ), f32),
            pltpu.VMEM((2, 16, LZ), f32),
            pltpu.VMEM((2, 16, LZ), f32),
            pltpu.VMEM((2, 8, LZ), f32),
            pltpu.VMEM((16, LZ), f32),
            pltpu.SemaphoreType.DMA((8,)),
            pltpu.SemaphoreType.DMA((8,)),
            pltpu.SemaphoreType.DMA((8,)),
            pltpu.SemaphoreType.REGULAR,
            pltpu.SemaphoreType.REGULAR,
        ],
        compiler_params=pltpu.CompilerParams(collective_id=0, has_side_effects=True, vmem_limit_bytes=32 * 2**20),
    )(flat, *operands)
    return out.reshape(3, LX, 1, LZ)


def solution(mesh):
    counts = (mesh.shape["gx"], mesh.shape["gz"])
    return jax.shard_map(
        lambda velocity: per_device(counts, velocity),
        mesh=mesh,
        in_specs=(P(None, "gx", None, "gz"),),
        out_specs=P(None, "gx", None, "gz"),
        check_vma=False,
    )
```

```python
import jax
import jax.numpy as jnp
import ml_dtypes
import numpy as np
from jax import lax
from jax.experimental import pallas as pl
from jax.experimental.pallas import tpu as pltpu
from jax.sharding import PartitionSpec as P

ALPHA_D = 1.0 / 3.0
COEF_A = 14.0 / 9.0
COEF_B = 1.0 / 9.0
ALPHA_F = 0.49
LX = 256
LZ = 128
EDGE = 96
EARLY = 3
SEAM = 8
MESH = pl.DeviceIdType.MESH


def filter_coefficients():
    return (
        (11.0 + 10.0 * ALPHA_F) / 16.0,
        (15.0 + 34.0 * ALPHA_F) / 32.0,
        (-3.0 + 6.0 * ALPHA_F) / 16.0,
        (1.0 - 2.0 * ALPHA_F) / 32.0,
    )


def line_kernel(alpha, stencil):
    root = np.sqrt(1.0 - 4.0 * alpha * alpha)
    rate = (-1.0 + root) / (2.0 * alpha)

    def response(n):
        n = np.asarray(n)
        return sum(s * rate ** np.abs(n + m) / root for m, s in stencil.items())

    far = max(stencil)
    return response, rate, float(response(far) / rate**far)


def slope_kernel():
    a, b = 0.5 * COEF_A, 0.25 * COEF_B
    response, rate, factor = line_kernel(ALPHA_D, {1: 0.5 * a, -1: -0.5 * a, 2: 0.5 * b, -2: -0.5 * b})
    return response, rate, factor, float(response(1)) - factor * rate


def smooth_kernel():
    c = filter_coefficients()
    stencil = {0: -c[0]}
    for n in (1, 2, 3):
        stencil[n] = stencil[-n] = -0.5 * c[n]
    response, rate, factor = line_kernel(ALPHA_F, stencil)
    near = [float(response(n)) - factor * rate**n for n in (1, 2)]
    return response, rate, factor, near


def halves(table):
    table = np.asarray(table, np.float32)
    high = table.astype(ml_dtypes.bfloat16)
    low = (table - high.astype(np.float32)).astype(ml_dtypes.bfloat16)
    return high, low


def tables():
    response, rate, factor, near = slope_kernel()
    i = np.arange(LX)
    k = np.arange(LZ)
    slope_x = np.concatenate(halves(response(i[:, None] - i[None, :])))
    high, low = halves(response(k[None, :] - k[:, None]))
    slope_z = np.block([[high, low], [high, np.zeros_like(low)]])
    sends = np.zeros((8, LZ))
    sends[0] = factor * rate ** (LZ - k)
    sends[1, LZ - 1] = 1.0
    sends[2] = -factor * rate ** (k + 1.0)
    sends[3, 0] = 1.0
    high, low = halves(sends)
    send_z = np.block([[high, high], [low, np.zeros_like(low)]])
    spread = np.zeros((32, 6, LZ))
    for f in range(6):
        spread[2 * f, f] = rate**k
        spread[2 * f + 1, f, 0] = near
        spread[16 + 2 * f, f] = rate ** (LZ - 1.0 - k)
        spread[17 + 2 * f, f, LZ - 1] = -near
    high, low = halves(spread.reshape(32, 6 * LZ))
    spread_z = np.concatenate([high, high, low])
    fade_x = np.zeros((2, EDGE, LZ), np.float32)
    fade_x[0] = (rate ** i[:EDGE])[:, None]
    fade_x[1] = fade_x[0, ::-1]
    response, rate, factor, _ = smooth_kernel()
    smooth_x = np.concatenate(halves(response(i[:, None] - i[None, :])))
    fade_f = np.zeros((2, LX, LZ), np.float32)
    fade_f[0] = (rate**i)[:, None]
    fade_f[1] = fade_f[0, ::-1]
    return fade_x, send_z, slope_x, slope_z, spread_z, fade_f, smooth_x


def split(values):
    high = values.astype(jnp.bfloat16)
    low = (values - high.astype(jnp.float32)).astype(jnp.bfloat16)
    return high, low


def dot(a, b, dims=((1,), (0,))):
    return lax.dot_general(a, b, (dims, ((), ())), preferred_element_type=jnp.float32)


def total(values):
    return jnp.sum(values, axis=0, keepdims=True)


def kernel(
    counts,
    velocity_hbm, fade_x_hbm, send_z_hbm, slope_x_hbm, slope_z_hbm, spread_z_hbm, fade_f_hbm, smooth_x_hbm,
    out,
    v, fade_x, send_z, slope_x, slope_z, spread_z, fade_f, smooth_x,
    fields, part_x, h, h_halves,
    z_out, z_in, z_use, z_far, w_far, x_out, x_in, x_use, x_far, f_out, f_in, ends, extra,
    load_sem, send_sem, recv_sem, ready, token,
):
    nx, nz = counts
    gx, gz = lax.axis_index("gx"), lax.axis_index("gz")
    x_next, x_prev = lax.rem(gx + 1, nx), lax.rem(gx + nx - 1, nx)
    z_next, z_prev = lax.rem(gz + 1, nz), lax.rem(gz + nz - 1, nz)
    sides_z = ((gx, z_next), (gx, z_prev))
    sides_x = ((x_next, gz), (x_prev, gz))
    is_first, is_last = gx == 0, gx == nx - 1
    ahead = jnp.logical_or(lax.rem(gz, SEAM) == SEAM - 1, gz == 1)
    behind = jnp.logical_or(lax.rem(gz, SEAM) == 0, gz == 2)
    is_second_last = gx == nx - 2
    last_ahead, last_behind = jnp.logical_and(is_last, ahead), jnp.logical_and(is_last, behind)
    last_seam = jnp.logical_or(last_ahead, last_behind)
    first_seam = jnp.logical_and(is_first, jnp.logical_or(ahead, behind))

    def signal(semaphore, side):
        pl.semaphore_signal(semaphore, inc=1, device_id=side, device_id_type=MESH)

    def remote(source, target, n, side):
        return pltpu.make_async_remote_copy(
            src_ref=source,
            dst_ref=target,
            send_sem=send_sem.at[n],
            recv_sem=recv_sem.at[n],
            device_id=side,
            device_id_type=MESH,
        )

    loads = [
        pltpu.make_async_copy(src, dst, load_sem.at[n])
        for n, (src, dst) in enumerate(
            (
                (velocity_hbm, v),
                (fade_x_hbm, fade_x),
                (send_z_hbm, send_z),
                (slope_x_hbm, slope_x),
                (slope_z_hbm, slope_z),
                (spread_z_hbm, spread_z),
                (fade_f_hbm, fade_f),
                (smooth_x_hbm, smooth_x),
            )
        )
    ]
    for load in loads[:EARLY]:
        load.start()

    z_use[...] = jnp.zeros_like(z_use)
    z_far[...] = jnp.zeros_like(z_far)
    x_use[...] = jnp.zeros_like(x_use)
    x_far[...] = jnp.zeros_like(x_far)
    extra[...] = jnp.zeros_like(extra)
    barrier = pltpu.get_barrier_semaphore()
    signal(barrier, sides_z[1])

    @pl.when(jnp.logical_not(last_ahead))
    def _():
        signal(barrier, sides_z[0])

    @pl.when(jnp.logical_not(is_first))
    def _():
        signal(barrier, sides_x[1])

    @pl.when(jnp.logical_not(is_last))
    def _():
        signal(barrier, sides_x[0])

    z_out[...] = jnp.zeros_like(z_out)
    for load in loads[:3]:
        load.wait()
    for load in loads[EARLY:]:
        load.start()
    u, w = v[0], v[2]
    values = (u * u, u * v[1], u, v[1], w, u * w, w * v[1], w * w)
    for n in (2, 3, 4, 5, 6, 7, 0, 1):
        high, low = split(values[n])
        fields[:, n * 256 : n * 256 + 128] = high
        fields[:, n * 256 + 128 : n * 256 + 256] = low

    for f in range(6):
        both = dot(send_z[...], fields[:, (2 + f) * 256 : (3 + f) * 256], ((1,), (1,)))
        both = both[:8] + both[8:]
        z_out[2 * f : 2 * f + 2] = both[0:2]
        z_out[16 + 2 * f : 18 + 2 * f] = both[2:4]

    rate_d, factor_d, near_d = slope_kernel()[1:]
    for side, row in ((0, LX - 1), (1, 0)):
        rows = slice(LX - EDGE, LX) if side == 0 else slice(0, EDGE)
        scale = factor_d * rate_d if side == 0 else -factor_d * rate_d
        for f in range(6):
            x_out[side, f : f + 1] = scale * total(fade_x[1 - side] * values[f][rows])
            x_out[side, 6 + f : 7 + f] = values[f][row : row + 1]

    fewer = jnp.where(jnp.logical_or(is_first, last_behind), 1, 0)
    pl.semaphore_wait(barrier, 4 - fewer + jnp.where(is_second_last, 1, 0))

    @pl.when(last_ahead)
    def _():
        signal(token, sides_z[0])

    @pl.when(is_last)
    def _():
        signal(ready, sides_x[0])

    @pl.when(is_first)
    def _():
        signal(barrier, sides_x[1])
        signal(barrier, (nx - 2, gz))

    halves_z = [pl.ds(16 * n, 16) for n in (0, 1)]
    copies = [remote(z_out.at[halves_z[n]], z_in.at[halves_z[n]], n, sides_z[n]) for n in (0, 1)]
    copies += [remote(x_out.at[n], x_in.at[n], 2 + n, sides_x[n]) for n in (0, 1)]
    copies += [remote(f_out.at[n], f_in.at[n], 4 + n, sides_x[n]) for n in (0, 1)]
    far = [remote(z_out.at[halves_z[n]], z_far.at[halves_z[n]], 6, (x_next, sides_z[n][1])) for n in (0, 1)]
    far_w = remote(v.at[2], w_far, 7, sides_x[0])
    far_x = remote(x_out.at[0], x_far, 8, (0, gz))
    copies[0].start()

    @pl.when(jnp.logical_not(last_behind))
    def _():
        copies[1].start()

    @pl.when(last_ahead)
    def _():
        far[0].start()

    @pl.when(last_behind)
    def _():
        far[1].start()

    copies[2].start()

    @pl.when(is_second_last)
    def _():
        far_x.start()

    @pl.when(jnp.logical_not(is_first))
    def _():
        copies[3].start()

    @pl.when(jnp.logical_and(last_seam, gz != 0))
    def _():
        far_w.start()

    loads[3].wait()
    loads[4].wait()
    flat = (0, 1, 5)
    for f in range(6):
        full = dot(slope_x[...], fields[:, f * 256 : f * 256 + 256])
        part_x[f] = full[:LX, :128] + full[:LX, 128:] + full[LX:, :128]
    for c in range(3):
        value = part_x[flat[c]] + v[0] * part_x[2 + c]
        for f, by_w in ((2 + c, True), (5 + c, False)):
            full = dot(fields[:, f * 256 : f * 256 + 256], slope_z[...])
            part = full[:, :128] + full[:, 128:]
            value = value + (v[2] * part if by_w else part)
        h[c] = value

    for load in loads[5:]:
        load.wait()

    top, end = slice(0, EDGE), slice(LX - EDGE, LX)
    f_out[0, 9:10] = total(fade_f[1, end] * (fade_x[1] * v[0, end]))
    f_out[0, 10:11] = v[0, LX - 1 : LX]
    f_out[0, 11:12] = v[0, LX - 2 : LX - 1]
    f_out[1, 9:10] = total(fade_f[0, top] * (fade_x[0] * v[0, top]))
    f_out[1, 10:11] = v[0, 0:1]
    f_out[1, 11:12] = v[0, 1:2]
    f_out[0, 13:14] = v[0, 0:1]
    moments = (
        total(fade_f[1, top] * (fade_x[0] * v[0, top])),
        total(fade_f[0, end] * (fade_x[1] * v[0, end])),
    )
    f_out[0, 12:13] = moments[0]
    rate_f, factor_f, (near1, near2) = smooth_kernel()[1:]
    powers = np.arange(EDGE, dtype=np.float64)
    near_sum = float(np.sum((rate_f * rate_d) ** powers))
    far_sum = float(np.sum(rate_f ** (LX - 1 - powers) * rate_d**powers))
    far_end = float(rate_f ** (LX - 1))

    def spread_of(sums, w_cells):
        high, low = split(sums)
        spread = dot(jnp.concatenate([high, low, high]), spread_z[...], ((0,), (0,)))
        return [spread[:, n * 128 + 384 : n * 128 + 512] + w_cells * spread[:, n * 128 : n * 128 + 128] for n in range(3)]

    @pl.when(jnp.logical_and(last_seam, gz == 0))
    def _():
        far_w.start()

    @pl.when(jnp.logical_not(last_behind))
    def _():
        copies[0].wait_recv()
        z_use[0:16] = z_in[0:16]

    @pl.when(jnp.logical_not(last_ahead))
    def _():
        copies[1].wait_recv()
        z_use[16:32] = z_in[16:32]

    for c, part in enumerate(spread_of(z_use[...], v[2])):
        value = h[c] + part
        h[c] = value
        ends[0, c : c + 1] = total(fade_f[1] * value)
        ends[1, c : c + 1] = total(fade_f[0] * value)

    first = lax.broadcasted_iota(jnp.int32, (8, LZ), 0) == 0
    last = lax.broadcasted_iota(jnp.int32, (8, LZ), 0) == 7
    for side, (edge, row0, row1) in enumerate(((0, LX - 1, LX - 2), (LX - 1, 0, 1))):
        if side == 1:

            @pl.when(is_first)
            def _():
                pl.semaphore_wait(ready, 1)
                copies[3].start()

            @pl.when(last_behind)
            def _():
                pl.semaphore_wait(token, 1)
                copies[1].start()
                copies[0].wait_recv()
                z_use[0:16] = z_in[0:16]
                z_use[16:32] = jnp.zeros_like(z_use[16:32])

            @pl.when(last_ahead)
            def _():
                copies[1].wait_recv()
                z_use[16:32] = z_in[16:32]
                z_use[0:16] = jnp.zeros_like(z_use[0:16])

            @pl.when(last_seam)
            def _():
                for c, part in enumerate(spread_of(z_use[...], v[2])):
                    value = h[c] + part
                    h[c] = value
                    ends[1, c : c + 1] = total(fade_f[0] * value)

            copies[3].wait_recv()
            x_use[1] = x_in[1]
        else:

            @pl.when(jnp.logical_not(is_last))
            def _():
                copies[2].wait_recv()
                x_use[0] = x_in[0]

        sign = near_d if side == 0 else -near_d
        for c in range(3):
            uv, vc = flat[c], 2 + c
            from_far = far_sum * x_use[side, uv : uv + 1] + moments[side] * x_use[side, vc : vc + 1]
            cell = x_use[side, 6 + uv : 7 + uv] + v[0, edge : edge + 1] * x_use[side, 6 + vc : 7 + vc]
            f_out[side, c : c + 1] = ends[side, c : c + 1] + from_far + (sign * far_end) * cell
            f_out[side, 3 + c : 4 + c] = h[c, row0 : row0 + 1]
            f_out[side, 6 + c : 7 + c] = h[c, row1 : row1 + 1]
        copies[4 + side].start()

    @pl.when(is_last)
    def _():
        copies[2].wait_recv()

    for c in range(3):
        uv, vc = flat[c], 2 + c
        h[c, top] += fade_x[0] * (x_in[0, uv : uv + 1] + v[0, top] * x_in[0, vc : vc + 1])
        cell = x_in[0, 6 + uv : 7 + uv] + v[0, 0:8] * x_in[0, 6 + vc : 7 + vc]
        h[c, 0:8] += jnp.where(first, near_d * cell, 0.0)
        h[c, end] += fade_x[1] * (x_in[1, uv : uv + 1] + v[0, end] * x_in[1, vc : vc + 1])
        cell = x_in[1, 6 + uv : 7 + uv] + v[0, LX - 8 : LX] * x_in[1, 6 + vc : 7 + vc]
        h[c, LX - 8 : LX] -= jnp.where(last, near_d * cell, 0.0)

    for c in range(3):
        high, low = split(h[c])
        h_halves[c, :, :128] = high
        h_halves[c, :, 128:] = low
        full = dot(smooth_x[...], h_halves[c])
        out[c] = full[:LX, :128] + full[:LX, 128:] + full[LX:, :128]

    @pl.when(is_first)
    def _():
        far_x.wait_recv()

    @pl.when(first_seam)
    def _():
        far[0].wait_recv()
        far_w.wait_recv()
        for c, part in enumerate(spread_of(z_far[...], w_far[...])):
            extra[c : c + 1] = total(fade_f[1] * part)
            extra[3 + c : 4 + c] = part[LX - 1 : LX]
            extra[6 + c : 7 + c] = part[LX - 2 : LX - 1]

    row = lax.broadcasted_iota(jnp.int32, (8, LZ), 0)
    copies[5].wait_recv()
    copies[4].wait_recv()
    scale = rate_f * factor_f
    for c in range(3):
        uv, vc = flat[c], 2 + c
        sums = []
        for side, sign, start, end0, end1 in ((0, -near_d, 0, 0, 1), (1, near_d, LX - 8, 7, 6)):
            own, own_v = x_out[1 - side, uv : uv + 1], x_out[1 - side, vc : vc + 1]
            edge, edge_v = x_out[1 - side, 6 + uv : 7 + uv], x_out[1 - side, 6 + vc : 7 + vc]
            moment, u1, u2 = (f_in[side, n : n + 1] for n in (9, 10, 11))
            sent = [f_in[side, n : n + 1] + (extra[n : n + 1] if side == 0 else 0.0) for n in (c, 3 + c, 6 + c)]
            cell = sign * (edge + u1 * edge_v)
            if side == 0:
                cell_far = x_far[6 + uv : 7 + uv] + f_in[0, 13:14] * x_far[6 + vc : 7 + vc]
                from_far = far_sum * x_far[uv : uv + 1] + f_in[0, 12:13] * x_far[vc : vc + 1]
                sent[0] += from_far + (near_d * far_end) * cell_far
            sums.append(scale * (sent[0] + near_sum * own + moment * own_v + cell))
            cell1 = sent[1] + own + u1 * own_v + cell
            cell2 = sent[2] + rate_d * (own + u2 * own_v)
            out[c, start : start + 8] += jnp.where(row == end0, near1 * cell1 + near2 * cell2, 0.0) + jnp.where(
                row == end1, near2 * cell1, 0.0
            )
        out[c] += fade_f[0] * sums[0] + fade_f[1] * sums[1]
    for copy in copies:
        copy.wait_send()

    @pl.when(is_second_last)
    def _():
        far_x.wait_send()

    @pl.when(last_seam)
    def _():
        far[0].wait_send()
        far_w.wait_send()


def per_device(counts, velocity):
    operands = [pltpu.with_memory_space_constraint(jnp.asarray(t), pltpu.HBM) for t in tables()]
    bf16, f32 = jnp.bfloat16, jnp.float32
    flat = pltpu.with_memory_space_constraint(velocity.reshape(3, LX, LZ), pltpu.HBM)
    out = pl.pallas_call(
        lambda *refs: kernel(counts, *refs),
        out_shape=jax.ShapeDtypeStruct((3, LX, LZ), f32),
        in_specs=[pl.BlockSpec(memory_space=pltpu.HBM)] * 8,
        out_specs=pl.BlockSpec(memory_space=pltpu.VMEM),
        scratch_shapes=[pltpu.VMEM((3, LX, LZ), f32)]
        + [pltpu.VMEM(t.shape, t.dtype) for t in operands]
        + [
            pltpu.VMEM((LX, 8 * 256), bf16),
            pltpu.VMEM((6, LX, LZ), f32),
            pltpu.VMEM((3, LX, LZ), f32),
            pltpu.VMEM((3, LX, 2 * LZ), bf16),
            pltpu.VMEM((32, LX), f32),
            pltpu.VMEM((32, LX), f32),
            pltpu.VMEM((32, LX), f32),
            pltpu.VMEM((32, LX), f32),
            pltpu.VMEM((LX, LZ), f32),
            pltpu.VMEM((2, 16, LZ), f32),
            pltpu.VMEM((2, 16, LZ), f32),
            pltpu.VMEM((2, 16, LZ), f32),
            pltpu.VMEM((16, LZ), f32),
            pltpu.VMEM((2, 16, LZ), f32),
            pltpu.VMEM((2, 16, LZ), f32),
            pltpu.VMEM((2, 8, LZ), f32),
            pltpu.VMEM((16, LZ), f32),
            pltpu.SemaphoreType.DMA((8,)),
            pltpu.SemaphoreType.DMA((9,)),
            pltpu.SemaphoreType.DMA((9,)),
            pltpu.SemaphoreType.REGULAR,
            pltpu.SemaphoreType.REGULAR,
        ],
        compiler_params=pltpu.CompilerParams(collective_id=0, has_side_effects=True, vmem_limit_bytes=32 * 2**20),
    )(flat, *operands)
    return out.reshape(3, LX, 1, LZ)


def solution(mesh):
    counts = (mesh.shape["gx"], mesh.shape["gz"])
    return jax.shard_map(
        lambda velocity: per_device(counts, velocity),
        mesh=mesh,
        in_specs=(P(None, "gx", None, "gz"),),
        out_specs=P(None, "gx", None, "gz"),
        check_vma=False,
    )
```

```python
import jax
import jax.numpy as jnp
import ml_dtypes
import numpy as np
from jax import lax
from jax.experimental import pallas as pl
from jax.experimental.pallas import tpu as pltpu
from jax.sharding import PartitionSpec as P

ALPHA_D = 1.0 / 3.0
COEF_A = 14.0 / 9.0
COEF_B = 1.0 / 9.0
ALPHA_F = 0.49
LX = 256
LZ = 128
EDGE = 96
EARLY = 3
SEAM = 8
MESH = pl.DeviceIdType.MESH


def filter_coefficients():
    return (
        (11.0 + 10.0 * ALPHA_F) / 16.0,
        (15.0 + 34.0 * ALPHA_F) / 32.0,
        (-3.0 + 6.0 * ALPHA_F) / 16.0,
        (1.0 - 2.0 * ALPHA_F) / 32.0,
    )


def line_kernel(alpha, stencil):
    root = np.sqrt(1.0 - 4.0 * alpha * alpha)
    rate = (-1.0 + root) / (2.0 * alpha)

    def response(n):
        n = np.asarray(n)
        return sum(s * rate ** np.abs(n + m) / root for m, s in stencil.items())

    far = max(stencil)
    return response, rate, float(response(far) / rate**far)


def slope_kernel():
    a, b = 0.5 * COEF_A, 0.25 * COEF_B
    response, rate, factor = line_kernel(ALPHA_D, {1: 0.5 * a, -1: -0.5 * a, 2: 0.5 * b, -2: -0.5 * b})
    return response, rate, factor, float(response(1)) - factor * rate


def smooth_kernel():
    c = filter_coefficients()
    stencil = {0: -c[0]}
    for n in (1, 2, 3):
        stencil[n] = stencil[-n] = -0.5 * c[n]
    response, rate, factor = line_kernel(ALPHA_F, stencil)
    near = [float(response(n)) - factor * rate**n for n in (1, 2)]
    return response, rate, factor, near


def halves(table):
    table = np.asarray(table, np.float32)
    high = table.astype(ml_dtypes.bfloat16)
    low = (table - high.astype(np.float32)).astype(ml_dtypes.bfloat16)
    return high, low


def tables():
    response, rate, factor, near = slope_kernel()
    i = np.arange(LX)
    k = np.arange(LZ)
    slope_x = np.concatenate(halves(response(i[:, None] - i[None, :])))
    high, low = halves(response(k[None, :] - k[:, None]))
    slope_z = np.block([[high, low], [high, np.zeros_like(low)]])
    sends = np.zeros((8, LZ))
    sends[0] = factor * rate ** (LZ - k)
    sends[1, LZ - 1] = 1.0
    sends[2] = -factor * rate ** (k + 1.0)
    sends[3, 0] = 1.0
    high, low = halves(sends)
    send_z = np.block([[high, high], [low, np.zeros_like(low)]])
    spread = np.zeros((32, 6, LZ))
    for f in range(6):
        spread[2 * f, f] = rate**k
        spread[2 * f + 1, f, 0] = near
        spread[16 + 2 * f, f] = rate ** (LZ - 1.0 - k)
        spread[17 + 2 * f, f, LZ - 1] = -near
    basis = np.stack([spread[:, :3].sum(axis=1), spread[:, 3:].sum(axis=1)]).astype(np.float32)
    high, low = halves(spread.reshape(32, 6 * LZ))
    spread_z = np.concatenate([high, high, low])
    fade_x = np.zeros((2, EDGE, LZ), np.float32)
    fade_x[0] = (rate ** i[:EDGE])[:, None]
    fade_x[1] = fade_x[0, ::-1]
    response, rate, factor, _ = smooth_kernel()
    smooth_x = np.concatenate(halves(response(i[:, None] - i[None, :])))
    fade_f = np.zeros((2, LX, LZ), np.float32)
    fade_f[0] = (rate**i)[:, None]
    fade_f[1] = fade_f[0, ::-1]
    return fade_x, send_z, slope_x, slope_z, spread_z, fade_f, smooth_x, basis


def split(values):
    high = values.astype(jnp.bfloat16)
    low = (values - high.astype(jnp.float32)).astype(jnp.bfloat16)
    return high, low


def dot(a, b, dims=((1,), (0,))):
    return lax.dot_general(a, b, (dims, ((), ())), preferred_element_type=jnp.float32)


def total(values):
    return jnp.sum(values, axis=0, keepdims=True)


def kernel(
    counts,
    velocity_hbm, fade_x_hbm, send_z_hbm, slope_x_hbm, slope_z_hbm, spread_z_hbm, fade_f_hbm, smooth_x_hbm, basis_hbm,
    out,
    v, fade_x, send_z, slope_x, slope_z, spread_z, fade_f, smooth_x, basis,
    fields, weights, part_x, h, h_halves,
    z_out, z_in, z_use, z_far, w_far, x_out, x_in, x_use, x_far, f_out, f_in, ends, extra,
    load_sem, send_sem, recv_sem, ready, token,
):
    nx, nz = counts
    gx, gz = lax.axis_index("gx"), lax.axis_index("gz")
    x_next, x_prev = lax.rem(gx + 1, nx), lax.rem(gx + nx - 1, nx)
    z_next, z_prev = lax.rem(gz + 1, nz), lax.rem(gz + nz - 1, nz)
    sides_z = ((gx, z_next), (gx, z_prev))
    sides_x = ((x_next, gz), (x_prev, gz))
    is_first, is_last = gx == 0, gx == nx - 1
    ahead = jnp.logical_or(lax.rem(gz, SEAM) == SEAM - 1, gz == 1)
    behind = jnp.logical_or(lax.rem(gz, SEAM) == 0, gz == 2)
    is_second_last = gx == nx - 2
    last_ahead, last_behind = jnp.logical_and(is_last, ahead), jnp.logical_and(is_last, behind)
    last_seam = jnp.logical_or(last_ahead, last_behind)
    first_seam = jnp.logical_and(is_first, jnp.logical_or(ahead, behind))

    def signal(semaphore, side):
        pl.semaphore_signal(semaphore, inc=1, device_id=side, device_id_type=MESH)

    def remote(source, target, n, side):
        return pltpu.make_async_remote_copy(
            src_ref=source,
            dst_ref=target,
            send_sem=send_sem.at[n],
            recv_sem=recv_sem.at[n],
            device_id=side,
            device_id_type=MESH,
        )

    loads = [
        pltpu.make_async_copy(src, dst, load_sem.at[n])
        for n, (src, dst) in enumerate(
            (
                (velocity_hbm, v),
                (fade_x_hbm, fade_x),
                (send_z_hbm, send_z),
                (slope_x_hbm, slope_x),
                (slope_z_hbm, slope_z),
                (spread_z_hbm, spread_z),
                (fade_f_hbm, fade_f),
                (smooth_x_hbm, smooth_x),
                (basis_hbm, basis),
            )
        )
    ]
    for load in loads[:EARLY]:
        load.start()

    z_use[...] = jnp.zeros_like(z_use)
    z_far[...] = jnp.zeros_like(z_far)
    x_use[...] = jnp.zeros_like(x_use)
    x_far[...] = jnp.zeros_like(x_far)
    extra[...] = jnp.zeros_like(extra)
    barrier = pltpu.get_barrier_semaphore()
    signal(barrier, sides_z[1])

    @pl.when(jnp.logical_not(last_ahead))
    def _():
        signal(barrier, sides_z[0])

    @pl.when(jnp.logical_not(is_first))
    def _():
        signal(barrier, sides_x[1])

    @pl.when(jnp.logical_not(is_last))
    def _():
        signal(barrier, sides_x[0])

    z_out[...] = jnp.zeros_like(z_out)
    for load in loads[:3]:
        load.wait()
    for load in loads[EARLY:]:
        load.start()
    u, w = v[0], v[2]
    values = (u * u, u * v[1], u, v[1], w, u * w, w * v[1], w * w)
    for n in (2, 3, 4, 5, 6, 7, 0, 1):
        high, low = split(values[n])
        fields[:, n * 256 : n * 256 + 128] = high
        fields[:, n * 256 + 128 : n * 256 + 256] = low

    for f in range(6):
        both = dot(send_z[...], fields[:, (2 + f) * 256 : (3 + f) * 256], ((1,), (1,)))
        both = both[:8] + both[8:]
        z_out[2 * f : 2 * f + 2] = both[0:2]
        z_out[16 + 2 * f : 18 + 2 * f] = both[2:4]

    fewer = jnp.where(jnp.logical_or(is_first, last_behind), 1, 0)
    pl.semaphore_wait(barrier, 4 - fewer + jnp.where(is_second_last, 1, 0))

    @pl.when(last_ahead)
    def _():
        signal(token, sides_z[0])

    @pl.when(is_last)
    def _():
        signal(ready, sides_x[0])

    @pl.when(is_first)
    def _():
        signal(barrier, sides_x[1])
        signal(barrier, (nx - 2, gz))

    halves_z = [pl.ds(16 * n, 16) for n in (0, 1)]
    copies = [remote(z_out.at[halves_z[n]], z_in.at[halves_z[n]], n, sides_z[n]) for n in (0, 1)]
    copies += [remote(x_out.at[n], x_in.at[n], 2 + n, sides_x[n]) for n in (0, 1)]
    copies += [remote(f_out.at[n], f_in.at[n], 4 + n, sides_x[n]) for n in (0, 1)]
    far = [remote(z_out.at[halves_z[n]], z_far.at[halves_z[n]], 6, (x_next, sides_z[n][1])) for n in (0, 1)]
    far_w = remote(v.at[2], w_far, 7, sides_x[0])
    far_x = remote(x_out.at[0], x_far, 8, (0, gz))
    @pl.when(last_ahead)
    def _():
        far[0].start()

    @pl.when(last_behind)
    def _():
        far[1].start()

    @pl.when(jnp.logical_not(last_behind))
    def _():
        copies[1].start()

    copies[0].start()

    rate_d, factor_d, near_d = slope_kernel()[1:]
    for side, row in ((0, LX - 1), (1, 0)):
        rows = slice(LX - EDGE, LX) if side == 0 else slice(0, EDGE)
        scale = factor_d * rate_d if side == 0 else -factor_d * rate_d
        for f in range(6):
            x_out[side, f : f + 1] = scale * total(fade_x[1 - side] * values[f][rows])
            x_out[side, 6 + f : 7 + f] = values[f][row : row + 1]

    copies[2].start()

    @pl.when(is_second_last)
    def _():
        far_x.start()

    @pl.when(jnp.logical_not(is_first))
    def _():
        copies[3].start()

    @pl.when(jnp.logical_and(last_seam, gz != 0))
    def _():
        far_w.start()

    loads[3].wait()
    loads[4].wait()
    flat = (0, 1, 5)
    for f in range(6):
        full = dot(slope_x[...], fields[:, f * 256 : f * 256 + 256])
        part_x[f] = full[:LX, :128] + full[:LX, 128:] + full[LX:, :128]
    for c in range(3):
        value = part_x[flat[c]] + v[0] * part_x[2 + c]
        for f, by_w in ((2 + c, True), (5 + c, False)):
            full = dot(fields[:, f * 256 : f * 256 + 256], slope_z[...])
            part = full[:, :128] + full[:, 128:]
            value = value + (v[2] * part if by_w else part)
        h[c] = value

    for load in loads[5:]:
        load.wait()

    top, end = slice(0, EDGE), slice(LX - EDGE, LX)
    f_out[0, 9:10] = total(fade_f[1, end] * (fade_x[1] * v[0, end]))
    f_out[0, 10:11] = v[0, LX - 1 : LX]
    f_out[0, 11:12] = v[0, LX - 2 : LX - 1]
    f_out[1, 9:10] = total(fade_f[0, top] * (fade_x[0] * v[0, top]))
    f_out[1, 10:11] = v[0, 0:1]
    f_out[1, 11:12] = v[0, 1:2]
    f_out[0, 13:14] = v[0, 0:1]
    moments = (
        total(fade_f[1, top] * (fade_x[0] * v[0, top])),
        total(fade_f[0, end] * (fade_x[1] * v[0, end])),
    )
    f_out[0, 12:13] = moments[0]
    rate_f, factor_f, (near1, near2) = smooth_kernel()[1:]
    powers = np.arange(EDGE, dtype=np.float64)
    near_sum = float(np.sum((rate_f * rate_d) ** powers))
    far_sum = float(np.sum(rate_f ** (LX - 1 - powers) * rate_d**powers))
    far_end = float(rate_f ** (LX - 1))

    def spread_of(sums, w_cells):
        high, low = split(sums)
        spread = dot(jnp.concatenate([high, low, high]), spread_z[...], ((0,), (0,)))
        return [spread[:, n * 128 + 384 : n * 128 + 512] + w_cells * spread[:, n * 128 : n * 128 + 128] for n in range(3)]

    def weigh(w_cells):
        high, low = split(fade_f[1] * w_cells)
        weights[:, :128] = high
        weights[:, 128:256] = low

    def message_of(sums, w_end):
        high, low = split(sums)
        full = dot(jnp.concatenate([high, low]), weights[...])
        by_w = full[:32, :128] + full[:32, 128:256] + full[32:, :128]
        plain = full[:32, 256:384] + full[:32, 384:] + full[32:, 256:384]
        terms = [basis[0] * by_w + basis[1] * plain]
        for n in (1, 2):
            cell = jnp.broadcast_to(sums[:, LX - n : LX - n + 1], (32, LZ))
            terms.append(cell * (basis[0] * w_end[8 - n : 9 - n] + basis[1]))
        both = [term[:16] + term[16:] for term in terms]
        return [
            [t[2 * c : 2 * c + 1] + t[2 * c + 1 : 2 * c + 2] + t[6 + 2 * c : 7 + 2 * c] + t[7 + 2 * c : 8 + 2 * c] for t in both]
            for c in range(3)
        ]

    high, low = split(fade_f[1])
    weights[:, 256:384] = high
    weights[:, 384:] = low
    weigh(v[2])
    for c in range(3):
        ends[0, c : c + 1] = total(fade_f[1] * h[c])

    @pl.when(jnp.logical_and(last_seam, gz == 0))
    def _():
        far_w.start()

    @pl.when(jnp.logical_not(last_behind))
    def _():
        copies[0].wait_recv()
        z_use[0:16] = z_in[0:16]

    @pl.when(jnp.logical_not(last_ahead))
    def _():
        copies[1].wait_recv()
        z_use[16:32] = z_in[16:32]

    @pl.when(jnp.logical_not(is_last))
    def _():
        copies[2].wait_recv()
        x_use[0] = x_in[0]

    first = lax.broadcasted_iota(jnp.int32, (8, LZ), 0) == 0
    last = lax.broadcasted_iota(jnp.int32, (8, LZ), 0) == 7

    def write_message(side, c, value, cell1, cell2):
        uv, vc = flat[c], 2 + c
        edge, sign = (0, near_d) if side == 0 else (LX - 1, -near_d)
        from_far = far_sum * x_use[side, uv : uv + 1] + moments[side] * x_use[side, vc : vc + 1]
        cell = x_use[side, 6 + uv : 7 + uv] + v[0, edge : edge + 1] * x_use[side, 6 + vc : 7 + vc]
        f_out[side, c : c + 1] = value + from_far + (sign * far_end) * cell
        f_out[side, 3 + c : 4 + c] = cell1
        f_out[side, 6 + c : 7 + c] = cell2

    for c, (value, cell1, cell2) in enumerate(message_of(z_use[...], v[2, LX - 8 : LX])):
        write_message(0, c, ends[0, c : c + 1] + value, h[c, LX - 1 : LX] + cell1, h[c, LX - 2 : LX - 1] + cell2)
    copies[4].start()

    for c, part in enumerate(spread_of(z_use[...], v[2])):
        h[c] += part

    @pl.when(is_first)
    def _():
        pl.semaphore_wait(ready, 1)
        copies[3].start()

    @pl.when(last_behind)
    def _():
        pl.semaphore_wait(token, 1)
        copies[1].start()
        copies[0].wait_recv()
        z_use[0:16] = z_in[0:16]
        z_use[16:32] = jnp.zeros_like(z_use[16:32])

    @pl.when(last_ahead)
    def _():
        copies[1].wait_recv()
        z_use[16:32] = z_in[16:32]
        z_use[0:16] = jnp.zeros_like(z_use[0:16])

    @pl.when(last_seam)
    def _():
        for c, part in enumerate(spread_of(z_use[...], v[2])):
            h[c] += part

    copies[3].wait_recv()
    x_use[1] = x_in[1]
    for c in range(3):
        write_message(1, c, total(fade_f[0] * h[c]), h[c, 0:1], h[c, 1:2])
    copies[5].start()

    @pl.when(is_last)
    def _():
        copies[2].wait_recv()

    for c in range(3):
        uv, vc = flat[c], 2 + c
        h[c, top] += fade_x[0] * (x_in[0, uv : uv + 1] + v[0, top] * x_in[0, vc : vc + 1])
        cell = x_in[0, 6 + uv : 7 + uv] + v[0, 0:8] * x_in[0, 6 + vc : 7 + vc]
        h[c, 0:8] += jnp.where(first, near_d * cell, 0.0)
        h[c, end] += fade_x[1] * (x_in[1, uv : uv + 1] + v[0, end] * x_in[1, vc : vc + 1])
        cell = x_in[1, 6 + uv : 7 + uv] + v[0, LX - 8 : LX] * x_in[1, 6 + vc : 7 + vc]
        h[c, LX - 8 : LX] -= jnp.where(last, near_d * cell, 0.0)

    for c in range(3):
        high, low = split(h[c])
        h_halves[c, :, :128] = high
        h_halves[c, :, 128:] = low
        full = dot(smooth_x[...], h_halves[c])
        out[c] = full[:LX, :128] + full[:LX, 128:] + full[LX:, :128]

    @pl.when(is_first)
    def _():
        far_x.wait_recv()

    @pl.when(first_seam)
    def _():
        far_w.wait_recv()
        weigh(w_far[...])
        far[0].wait_recv()
        for c, parts in enumerate(message_of(z_far[...], w_far[LX - 8 : LX])):
            for n, part in enumerate(parts):
                extra[3 * n + c : 3 * n + c + 1] = part

    row = lax.broadcasted_iota(jnp.int32, (8, LZ), 0)
    copies[5].wait_recv()
    copies[4].wait_recv()
    scale = rate_f * factor_f
    for c in range(3):
        uv, vc = flat[c], 2 + c
        sums = []
        for side, sign, start, end0, end1 in ((0, -near_d, 0, 0, 1), (1, near_d, LX - 8, 7, 6)):
            own, own_v = x_out[1 - side, uv : uv + 1], x_out[1 - side, vc : vc + 1]
            edge, edge_v = x_out[1 - side, 6 + uv : 7 + uv], x_out[1 - side, 6 + vc : 7 + vc]
            moment, u1, u2 = (f_in[side, n : n + 1] for n in (9, 10, 11))
            sent = [f_in[side, n : n + 1] + (extra[n : n + 1] if side == 0 else 0.0) for n in (c, 3 + c, 6 + c)]
            cell = sign * (edge + u1 * edge_v)
            if side == 0:
                cell_far = x_far[6 + uv : 7 + uv] + f_in[0, 13:14] * x_far[6 + vc : 7 + vc]
                from_far = far_sum * x_far[uv : uv + 1] + f_in[0, 12:13] * x_far[vc : vc + 1]
                sent[0] += from_far + (near_d * far_end) * cell_far
            sums.append(scale * (sent[0] + near_sum * own + moment * own_v + cell))
            cell1 = sent[1] + own + u1 * own_v + cell
            cell2 = sent[2] + rate_d * (own + u2 * own_v)
            out[c, start : start + 8] += jnp.where(row == end0, near1 * cell1 + near2 * cell2, 0.0) + jnp.where(
                row == end1, near2 * cell1, 0.0
            )
        out[c] += fade_f[0] * sums[0] + fade_f[1] * sums[1]
    for copy in copies:
        copy.wait_send()

    @pl.when(is_second_last)
    def _():
        far_x.wait_send()

    @pl.when(last_seam)
    def _():
        far[0].wait_send()
        far_w.wait_send()


def per_device(counts, velocity):
    operands = [pltpu.with_memory_space_constraint(jnp.asarray(t), pltpu.HBM) for t in tables()]
    bf16, f32 = jnp.bfloat16, jnp.float32
    flat = pltpu.with_memory_space_constraint(velocity.reshape(3, LX, LZ), pltpu.HBM)
    out = pl.pallas_call(
        lambda *refs: kernel(counts, *refs),
        out_shape=jax.ShapeDtypeStruct((3, LX, LZ), f32),
        in_specs=[pl.BlockSpec(memory_space=pltpu.HBM)] * 9,
        out_specs=pl.BlockSpec(memory_space=pltpu.VMEM),
        scratch_shapes=[pltpu.VMEM((3, LX, LZ), f32)]
        + [pltpu.VMEM(t.shape, t.dtype) for t in operands]
        + [
            pltpu.VMEM((LX, 8 * 256), bf16),
            pltpu.VMEM((LX, 4 * LZ), bf16),
            pltpu.VMEM((6, LX, LZ), f32),
            pltpu.VMEM((3, LX, LZ), f32),
            pltpu.VMEM((3, LX, 2 * LZ), bf16),
            pltpu.VMEM((32, LX), f32),
            pltpu.VMEM((32, LX), f32),
            pltpu.VMEM((32, LX), f32),
            pltpu.VMEM((32, LX), f32),
            pltpu.VMEM((LX, LZ), f32),
            pltpu.VMEM((2, 16, LZ), f32),
            pltpu.VMEM((2, 16, LZ), f32),
            pltpu.VMEM((2, 16, LZ), f32),
            pltpu.VMEM((16, LZ), f32),
            pltpu.VMEM((2, 16, LZ), f32),
            pltpu.VMEM((2, 16, LZ), f32),
            pltpu.VMEM((1, 8, LZ), f32),
            pltpu.VMEM((16, LZ), f32),
            pltpu.SemaphoreType.DMA((9,)),
            pltpu.SemaphoreType.DMA((9,)),
            pltpu.SemaphoreType.DMA((9,)),
            pltpu.SemaphoreType.REGULAR,
            pltpu.SemaphoreType.REGULAR,
        ],
        compiler_params=pltpu.CompilerParams(collective_id=0, has_side_effects=True, vmem_limit_bytes=32 * 2**20),
    )(flat, *operands)
    return out.reshape(3, LX, 1, LZ)


def solution(mesh):
    counts = (mesh.shape["gx"], mesh.shape["gz"])
    return jax.shard_map(
        lambda velocity: per_device(counts, velocity),
        mesh=mesh,
        in_specs=(P(None, "gx", None, "gz"),),
        out_specs=P(None, "gx", None, "gz"),
        check_vma=False,
    )
```

```python
import jax
import jax.numpy as jnp
import ml_dtypes
import numpy as np
from jax import lax
from jax.experimental import pallas as pl
from jax.experimental.pallas import tpu as pltpu
from jax.sharding import PartitionSpec as P

ALPHA_D = 1.0 / 3.0
COEF_A = 14.0 / 9.0
COEF_B = 1.0 / 9.0
ALPHA_F = 0.49
LX = 256
LZ = 128
EDGE = 96
PIECE = 256
SEAM = 8
MESH = pl.DeviceIdType.MESH


def filter_coefficients():
    return (
        (11.0 + 10.0 * ALPHA_F) / 16.0,
        (15.0 + 34.0 * ALPHA_F) / 32.0,
        (-3.0 + 6.0 * ALPHA_F) / 16.0,
        (1.0 - 2.0 * ALPHA_F) / 32.0,
    )


def line_kernel(alpha, stencil):
    root = np.sqrt(1.0 - 4.0 * alpha * alpha)
    rate = (-1.0 + root) / (2.0 * alpha)

    def response(n):
        n = np.asarray(n)
        return sum(s * rate ** np.abs(n + m) / root for m, s in stencil.items())

    far = max(stencil)
    return response, rate, float(response(far) / rate**far)


def slope_kernel():
    a, b = 0.5 * COEF_A, 0.25 * COEF_B
    response, rate, factor = line_kernel(ALPHA_D, {1: 0.5 * a, -1: -0.5 * a, 2: 0.5 * b, -2: -0.5 * b})
    return response, rate, factor, float(response(1)) - factor * rate


def smooth_kernel():
    c = filter_coefficients()
    stencil = {0: -c[0]}
    for n in (1, 2, 3):
        stencil[n] = stencil[-n] = -0.5 * c[n]
    response, rate, factor = line_kernel(ALPHA_F, stencil)
    near = [float(response(n)) - factor * rate**n for n in (1, 2)]
    return response, rate, factor, near


def halves(table):
    table = np.asarray(table, np.float32)
    high = table.astype(ml_dtypes.bfloat16)
    low = (table - high.astype(np.float32)).astype(ml_dtypes.bfloat16)
    return high, low


def tables():
    response, rate, factor, near = slope_kernel()
    i = np.arange(LX)
    k = np.arange(LZ)
    slope_x = np.concatenate(halves(response(i[:, None] - i[None, :])))
    high, low = halves(response(k[None, :] - k[:, None]))
    slope_z = np.block([[high, low], [high, np.zeros_like(low)]])
    sends = np.zeros((8, LZ))
    sends[0] = factor * rate ** (LZ - k)
    sends[1, LZ - 1] = 1.0
    sends[2] = -factor * rate ** (k + 1.0)
    sends[3, 0] = 1.0
    high, low = halves(sends)
    send_z = np.block([[high, high], [low, np.zeros_like(low)]])
    spread = np.zeros((32, 6, LZ))
    for f in range(6):
        spread[2 * f, f] = rate**k
        spread[2 * f + 1, f, 0] = near
        spread[16 + 2 * f, f] = rate ** (LZ - 1.0 - k)
        spread[17 + 2 * f, f, LZ - 1] = -near
    basis = np.stack([spread[:, :3].sum(axis=1), spread[:, 3:].sum(axis=1)]).astype(np.float32)
    high, low = halves(spread.reshape(32, 6 * LZ))
    spread_z = np.concatenate([high, high, low])
    fade_x = np.zeros((2, EDGE, LZ), np.float32)
    fade_x[0] = (rate ** i[:EDGE])[:, None]
    fade_x[1] = fade_x[0, ::-1]
    response, rate, factor, _ = smooth_kernel()
    smooth_x = np.concatenate(halves(response(i[:, None] - i[None, :])))
    fade_f = np.zeros((2, LX, LZ), np.float32)
    fade_f[0] = (rate**i)[:, None]
    fade_f[1] = fade_f[0, ::-1]
    return fade_x, send_z, slope_x, slope_z, spread_z, fade_f, smooth_x, basis


def split(values):
    high = values.astype(jnp.bfloat16)
    low = (values - high.astype(jnp.float32)).astype(jnp.bfloat16)
    return high, low


def dot(a, b, dims=((1,), (0,))):
    return lax.dot_general(a, b, (dims, ((), ())), preferred_element_type=jnp.float32)


def total(values):
    return jnp.sum(values, axis=0, keepdims=True)


def kernel(
    counts,
    velocity_hbm, fade_x_hbm, send_z_hbm, slope_x_hbm, slope_z_hbm, spread_z_hbm, fade_f_hbm, smooth_x_hbm, basis_hbm,
    out,
    v, fade_x, send_z, slope_x, slope_z, spread_z, fade_f, smooth_x, basis,
    fields, weights, part_x, h, h_halves,
    z_out, z_in, z_use, z_far, w_far, x_out, x_in, x_use, x_far, f_out, f_in, ends, extra,
    load_sem, send_sem, recv_sem, ready, token,
):
    nx, nz = counts
    gx, gz = lax.axis_index("gx"), lax.axis_index("gz")
    x_next, x_prev = lax.rem(gx + 1, nx), lax.rem(gx + nx - 1, nx)
    z_next, z_prev = lax.rem(gz + 1, nz), lax.rem(gz + nz - 1, nz)
    sides_z = ((gx, z_next), (gx, z_prev))
    sides_x = ((x_next, gz), (x_prev, gz))
    is_first, is_last = gx == 0, gx == nx - 1
    ahead = jnp.logical_or(lax.rem(gz, SEAM) == SEAM - 1, gz == 1)
    behind = jnp.logical_or(lax.rem(gz, SEAM) == 0, gz == 2)
    is_second_last = gx == nx - 2
    last_ahead, last_behind = jnp.logical_and(is_last, ahead), jnp.logical_and(is_last, behind)
    last_seam = jnp.logical_or(last_ahead, last_behind)
    first_seam = jnp.logical_and(is_first, jnp.logical_or(ahead, behind))

    def signal(semaphore, side):
        pl.semaphore_signal(semaphore, inc=1, device_id=side, device_id_type=MESH)

    def remote(source, target, n, side):
        return pltpu.make_async_remote_copy(
            src_ref=source,
            dst_ref=target,
            send_sem=send_sem.at[n],
            recv_sem=recv_sem.at[n],
            device_id=side,
            device_id_type=MESH,
        )

    loads = [
        pltpu.make_async_copy(src, dst, load_sem.at[n])
        for n, (src, dst) in enumerate(
            (
                (fade_x_hbm, fade_x),
                (send_z_hbm, send_z),
                (slope_x_hbm, slope_x),
                (slope_z_hbm, slope_z),
                (spread_z_hbm, spread_z),
                (fade_f_hbm, fade_f),
                (smooth_x_hbm, smooth_x),
                (basis_hbm, basis),
            )
        )
    ]
    pieces = [
        pltpu.make_async_copy(
            velocity_hbm.at[c, pl.ds(r * PIECE, PIECE)],
            v.at[c, pl.ds(r * PIECE, PIECE)],
            load_sem.at[len(loads) + c * (LX // PIECE) + r],
        )
        for c in range(3)
        for r in range(LX // PIECE)
    ]
    for load in pieces + loads[:2]:
        load.start()

    z_far[...] = jnp.zeros_like(z_far)
    x_far[...] = jnp.zeros_like(x_far)
    barrier = pltpu.get_barrier_semaphore()
    signal(barrier, sides_z[1])

    @pl.when(jnp.logical_not(last_ahead))
    def _():
        signal(barrier, sides_z[0])

    @pl.when(jnp.logical_not(is_first))
    def _():
        signal(barrier, sides_x[1])

    @pl.when(jnp.logical_not(is_last))
    def _():
        signal(barrier, sides_x[0])

    for ref in (z_out, z_use, x_use, extra):
        ref[...] = jnp.zeros_like(ref)
    for load in pieces + loads[1:2]:
        load.wait()
    for load in loads[2:]:
        load.start()
    u, w = v[0], v[2]
    values = (u * u, u * v[1], u, v[1], w, u * w, w * v[1], w * w)

    def store_field(n):
        high, low = split(values[n])
        fields[:, n * 256 : n * 256 + 128] = high
        fields[:, n * 256 + 128 : n * 256 + 256] = low

    for n in range(2, 8):
        store_field(n)

    for f in range(6):
        both = dot(send_z[...], fields[:, (2 + f) * 256 : (3 + f) * 256], ((1,), (1,)))
        both = both[:8] + both[8:]
        z_out[2 * f : 2 * f + 2] = both[0:2]
        z_out[16 + 2 * f : 18 + 2 * f] = both[2:4]

    fewer = jnp.where(jnp.logical_or(is_first, last_behind), 1, 0)
    pl.semaphore_wait(barrier, 4 - fewer + jnp.where(is_second_last, 1, 0))

    @pl.when(last_ahead)
    def _():
        signal(token, sides_z[0])

    @pl.when(is_last)
    def _():
        signal(ready, sides_x[0])

    @pl.when(is_first)
    def _():
        signal(barrier, sides_x[1])
        signal(barrier, (nx - 2, gz))

    halves_z = [pl.ds(16 * n, 16) for n in (0, 1)]
    copies = [remote(z_out.at[halves_z[n]], z_in.at[halves_z[n]], n, sides_z[n]) for n in (0, 1)]
    copies += [remote(x_out.at[n], x_in.at[n], 2 + n, sides_x[n]) for n in (0, 1)]
    copies += [remote(f_out.at[n], f_in.at[n], 4 + n, sides_x[n]) for n in (0, 1)]
    far = [remote(z_out.at[halves_z[n]], z_far.at[halves_z[n]], 6, (x_next, sides_z[n][1])) for n in (0, 1)]
    far_w = remote(v.at[2], w_far, 7, sides_x[0])
    far_x = remote(x_out.at[0], x_far, 8, (0, gz))
    @pl.when(last_ahead)
    def _():
        far[0].start()

    @pl.when(last_behind)
    def _():
        far[1].start()

    @pl.when(jnp.logical_not(last_behind))
    def _():
        copies[1].start()

    copies[0].start()

    loads[0].wait()
    rate_d, factor_d, near_d = slope_kernel()[1:]
    for side, row in ((0, LX - 1), (1, 0)):
        rows = slice(LX - EDGE, LX) if side == 0 else slice(0, EDGE)
        scale = factor_d * rate_d if side == 0 else -factor_d * rate_d
        for f in range(6):
            x_out[side, f : f + 1] = scale * total(fade_x[1 - side] * values[f][rows])
            x_out[side, 6 + f : 7 + f] = values[f][row : row + 1]

    copies[2].start()

    @pl.when(is_second_last)
    def _():
        far_x.start()

    @pl.when(jnp.logical_not(is_first))
    def _():
        copies[3].start()

    @pl.when(jnp.logical_and(last_seam, gz != 0))
    def _():
        far_w.start()

    for n in (0, 1):
        store_field(n)
    loads[2].wait()
    loads[3].wait()
    flat = (0, 1, 5)
    for f in range(6):
        full = dot(slope_x[...], fields[:, f * 256 : f * 256 + 256])
        part_x[f] = full[:LX, :128] + full[:LX, 128:] + full[LX:, :128]
    for c in range(3):
        value = part_x[flat[c]] + v[0] * part_x[2 + c]
        for f, by_w in ((2 + c, True), (5 + c, False)):
            full = dot(fields[:, f * 256 : f * 256 + 256], slope_z[...])
            part = full[:, :128] + full[:, 128:]
            value = value + (v[2] * part if by_w else part)
        h[c] = value

    for load in loads[4:]:
        load.wait()

    top, end = slice(0, EDGE), slice(LX - EDGE, LX)
    f_out[0, 9:10] = total(fade_f[1, end] * (fade_x[1] * v[0, end]))
    f_out[0, 10:11] = v[0, LX - 1 : LX]
    f_out[0, 11:12] = v[0, LX - 2 : LX - 1]
    f_out[1, 9:10] = total(fade_f[0, top] * (fade_x[0] * v[0, top]))
    f_out[1, 10:11] = v[0, 0:1]
    f_out[1, 11:12] = v[0, 1:2]
    f_out[0, 13:14] = v[0, 0:1]
    moments = (
        total(fade_f[1, top] * (fade_x[0] * v[0, top])),
        total(fade_f[0, end] * (fade_x[1] * v[0, end])),
    )
    f_out[0, 12:13] = moments[0]
    rate_f, factor_f, (near1, near2) = smooth_kernel()[1:]
    powers = np.arange(EDGE, dtype=np.float64)
    near_sum = float(np.sum((rate_f * rate_d) ** powers))
    far_sum = float(np.sum(rate_f ** (LX - 1 - powers) * rate_d**powers))
    far_end = float(rate_f ** (LX - 1))

    def spread_of(sums, w_cells):
        high, low = split(sums)
        spread = dot(jnp.concatenate([high, low, high]), spread_z[...], ((0,), (0,)))
        return [spread[:, n * 128 + 384 : n * 128 + 512] + w_cells * spread[:, n * 128 : n * 128 + 128] for n in range(3)]

    def weigh(w_cells):
        high, low = split(fade_f[1] * w_cells)
        weights[:, :128] = high
        weights[:, 128:256] = low

    def message_of(sums, w_end):
        high, low = split(sums)
        full = dot(jnp.concatenate([high, low]), weights[...])
        by_w = full[:32, :128] + full[:32, 128:256] + full[32:, :128]
        plain = full[:32, 256:384] + full[:32, 384:] + full[32:, 256:384]
        terms = [basis[0] * by_w + basis[1] * plain]
        for n in (1, 2):
            cell = jnp.broadcast_to(sums[:, LX - n : LX - n + 1], (32, LZ))
            terms.append(cell * (basis[0] * w_end[8 - n : 9 - n] + basis[1]))
        both = [term[:16] + term[16:] for term in terms]
        return [
            [t[2 * c : 2 * c + 1] + t[2 * c + 1 : 2 * c + 2] + t[6 + 2 * c : 7 + 2 * c] + t[7 + 2 * c : 8 + 2 * c] for t in both]
            for c in range(3)
        ]

    high, low = split(fade_f[1])
    weights[:, 256:384] = high
    weights[:, 384:] = low
    weigh(v[2])
    for c in range(3):
        ends[0, c : c + 1] = total(fade_f[1] * h[c])

    @pl.when(jnp.logical_and(last_seam, gz == 0))
    def _():
        far_w.start()

    @pl.when(jnp.logical_not(last_behind))
    def _():
        copies[0].wait_recv()
        z_use[0:16] = z_in[0:16]

    @pl.when(jnp.logical_not(last_ahead))
    def _():
        copies[1].wait_recv()
        z_use[16:32] = z_in[16:32]

    @pl.when(jnp.logical_not(is_last))
    def _():
        copies[2].wait_recv()
        x_use[0] = x_in[0]

    first = lax.broadcasted_iota(jnp.int32, (8, LZ), 0) == 0
    last = lax.broadcasted_iota(jnp.int32, (8, LZ), 0) == 7

    def write_message(side, c, value, cell1, cell2):
        uv, vc = flat[c], 2 + c
        edge, sign = (0, near_d) if side == 0 else (LX - 1, -near_d)
        from_far = far_sum * x_use[side, uv : uv + 1] + moments[side] * x_use[side, vc : vc + 1]
        cell = x_use[side, 6 + uv : 7 + uv] + v[0, edge : edge + 1] * x_use[side, 6 + vc : 7 + vc]
        f_out[side, c : c + 1] = value + from_far + (sign * far_end) * cell
        f_out[side, 3 + c : 4 + c] = cell1
        f_out[side, 6 + c : 7 + c] = cell2

    for c, (value, cell1, cell2) in enumerate(message_of(z_use[...], v[2, LX - 8 : LX])):
        write_message(0, c, ends[0, c : c + 1] + value, h[c, LX - 1 : LX] + cell1, h[c, LX - 2 : LX - 1] + cell2)
    copies[4].start()

    for c, part in enumerate(spread_of(z_use[...], v[2])):
        h[c] += part

    @pl.when(is_first)
    def _():
        pl.semaphore_wait(ready, 1)
        copies[3].start()

    @pl.when(last_behind)
    def _():
        pl.semaphore_wait(token, 1)
        copies[1].start()
        copies[0].wait_recv()
        z_use[0:16] = z_in[0:16]
        z_use[16:32] = jnp.zeros_like(z_use[16:32])

    @pl.when(last_ahead)
    def _():
        copies[1].wait_recv()
        z_use[16:32] = z_in[16:32]
        z_use[0:16] = jnp.zeros_like(z_use[0:16])

    @pl.when(last_seam)
    def _():
        for c, part in enumerate(spread_of(z_use[...], v[2])):
            h[c] += part

    copies[3].wait_recv()
    x_use[1] = x_in[1]
    for c in range(3):
        write_message(1, c, total(fade_f[0] * h[c]), h[c, 0:1], h[c, 1:2])
    copies[5].start()

    @pl.when(is_last)
    def _():
        copies[2].wait_recv()

    for c in range(3):
        uv, vc = flat[c], 2 + c
        h[c, top] += fade_x[0] * (x_in[0, uv : uv + 1] + v[0, top] * x_in[0, vc : vc + 1])
        cell = x_in[0, 6 + uv : 7 + uv] + v[0, 0:8] * x_in[0, 6 + vc : 7 + vc]
        h[c, 0:8] += jnp.where(first, near_d * cell, 0.0)
        h[c, end] += fade_x[1] * (x_in[1, uv : uv + 1] + v[0, end] * x_in[1, vc : vc + 1])
        cell = x_in[1, 6 + uv : 7 + uv] + v[0, LX - 8 : LX] * x_in[1, 6 + vc : 7 + vc]
        h[c, LX - 8 : LX] -= jnp.where(last, near_d * cell, 0.0)

    for c in range(3):
        high, low = split(h[c])
        h_halves[c, :, :128] = high
        h_halves[c, :, 128:] = low
        full = dot(smooth_x[...], h_halves[c])
        out[c] = full[:LX, :128] + full[:LX, 128:] + full[LX:, :128]

    @pl.when(is_first)
    def _():
        far_x.wait_recv()

    @pl.when(first_seam)
    def _():
        far_w.wait_recv()
        weigh(w_far[...])
        far[0].wait_recv()
        for c, parts in enumerate(message_of(z_far[...], w_far[LX - 8 : LX])):
            for n, part in enumerate(parts):
                extra[3 * n + c : 3 * n + c + 1] = part

    row = lax.broadcasted_iota(jnp.int32, (8, LZ), 0)
    copies[5].wait_recv()
    copies[4].wait_recv()
    scale = rate_f * factor_f
    for c in range(3):
        uv, vc = flat[c], 2 + c
        sums = []
        for side, sign, start, end0, end1 in ((0, -near_d, 0, 0, 1), (1, near_d, LX - 8, 7, 6)):
            own, own_v = x_out[1 - side, uv : uv + 1], x_out[1 - side, vc : vc + 1]
            edge, edge_v = x_out[1 - side, 6 + uv : 7 + uv], x_out[1 - side, 6 + vc : 7 + vc]
            moment, u1, u2 = (f_in[side, n : n + 1] for n in (9, 10, 11))
            sent = [f_in[side, n : n + 1] + (extra[n : n + 1] if side == 0 else 0.0) for n in (c, 3 + c, 6 + c)]
            cell = sign * (edge + u1 * edge_v)
            if side == 0:
                cell_far = x_far[6 + uv : 7 + uv] + f_in[0, 13:14] * x_far[6 + vc : 7 + vc]
                from_far = far_sum * x_far[uv : uv + 1] + f_in[0, 12:13] * x_far[vc : vc + 1]
                sent[0] += from_far + (near_d * far_end) * cell_far
            sums.append(scale * (sent[0] + near_sum * own + moment * own_v + cell))
            cell1 = sent[1] + own + u1 * own_v + cell
            cell2 = sent[2] + rate_d * (own + u2 * own_v)
            out[c, start : start + 8] += jnp.where(row == end0, near1 * cell1 + near2 * cell2, 0.0) + jnp.where(
                row == end1, near2 * cell1, 0.0
            )
        out[c] += fade_f[0] * sums[0] + fade_f[1] * sums[1]
    for copy in copies:
        copy.wait_send()

    @pl.when(is_second_last)
    def _():
        far_x.wait_send()

    @pl.when(last_seam)
    def _():
        far[0].wait_send()
        far_w.wait_send()


def per_device(counts, velocity):
    operands = [pltpu.with_memory_space_constraint(jnp.asarray(t), pltpu.HBM) for t in tables()]
    bf16, f32 = jnp.bfloat16, jnp.float32
    flat = pltpu.with_memory_space_constraint(velocity.reshape(3, LX, LZ), pltpu.HBM)
    out = pl.pallas_call(
        lambda *refs: kernel(counts, *refs),
        out_shape=jax.ShapeDtypeStruct((3, LX, LZ), f32),
        in_specs=[pl.BlockSpec(memory_space=pltpu.HBM)] * 9,
        out_specs=pl.BlockSpec(memory_space=pltpu.VMEM),
        scratch_shapes=[pltpu.VMEM((3, LX, LZ), f32)]
        + [pltpu.VMEM(t.shape, t.dtype) for t in operands]
        + [
            pltpu.VMEM((LX, 8 * 256), bf16),
            pltpu.VMEM((LX, 4 * LZ), bf16),
            pltpu.VMEM((6, LX, LZ), f32),
            pltpu.VMEM((3, LX, LZ), f32),
            pltpu.VMEM((3, LX, 2 * LZ), bf16),
            pltpu.VMEM((32, LX), f32),
            pltpu.VMEM((32, LX), f32),
            pltpu.VMEM((32, LX), f32),
            pltpu.VMEM((32, LX), f32),
            pltpu.VMEM((LX, LZ), f32),
            pltpu.VMEM((2, 16, LZ), f32),
            pltpu.VMEM((2, 16, LZ), f32),
            pltpu.VMEM((2, 16, LZ), f32),
            pltpu.VMEM((16, LZ), f32),
            pltpu.VMEM((2, 16, LZ), f32),
            pltpu.VMEM((2, 16, LZ), f32),
            pltpu.VMEM((1, 8, LZ), f32),
            pltpu.VMEM((16, LZ), f32),
            pltpu.SemaphoreType.DMA((8 + 3 * LX // PIECE,)),
            pltpu.SemaphoreType.DMA((9,)),
            pltpu.SemaphoreType.DMA((9,)),
            pltpu.SemaphoreType.REGULAR,
            pltpu.SemaphoreType.REGULAR,
        ],
        compiler_params=pltpu.CompilerParams(collective_id=0, has_side_effects=True, vmem_limit_bytes=32 * 2**20),
    )(flat, *operands)
    return out.reshape(3, LX, 1, LZ)


def solution(mesh):
    counts = (mesh.shape["gx"], mesh.shape["gz"])
    return jax.shard_map(
        lambda velocity: per_device(counts, velocity),
        mesh=mesh,
        in_specs=(P(None, "gx", None, "gz"),),
        out_specs=P(None, "gx", None, "gz"),
        check_vma=False,
    )
```
